512 devices in a mesh: tm: 32 (over z, y_lo), row: 16 (over x, y_hi, core).
Axes of the slice: x: 4, y: 8 (y_hi: 2, y_lo: 4; y = y_hi * 4 + y_lo), z: 8, core: 2. Of those that a mesh axis runs over, the one named last changes fastest.
Arguments:
- output_first_half: bfloat16 [64, 16, 64, 320], P('tm', 'row'), may hold values from -6 to 6
- y_second: bfloat16 [64, 16, 64, 320], P('tm', 'row'), may hold values from -6 to 6
- cot_first: bfloat16 [64, 16, 64, 320], P('tm', 'row'), may hold values from -6 to 6
- cot_second: bfloat16 [64, 16, 64, 320], P('tm', 'row'), may hold values from -6 to 6
- weight_space: bfloat16 [3, 3, 2, 160, 160], replicated, may hold values from -0.15625 to 0.15625
- temporal_weight: bfloat16 [3, 5, 128, 128], replicated, may hold values from -0.3125 to 0.3125
Outputs:
- x_first: bfloat16 [64, 16, 64, 320], P('tm', 'row')
- x_second: bfloat16 [64, 16, 64, 320], P('tm', 'row')
- grad_first: bfloat16 [64, 16, 64, 320], P('tm', 'row')
- grad_second: bfloat16 [64, 16, 64, 320], P('tm', 'row')
- spatial_weight_gradient: float32 [460800], P(('tm', 'row'))
- grad_time: float32 [245760], P(('tm', 'row'))
The draws below stay inside these ranges and needn't reach their ends.
All inputs are finite; a program needn't handle non-finite values.
Results may differ from the reference program's by a relative error of at most 0.007.
Values may be sent and summed in bfloat16 or wider, within the bound.
A program may use at most 64 MiB of HBM per device.

```python
import math
import jax
import jax.numpy as jnp
from jax import lax

CH = 320
GS = 160
GROUP_CHANNELS = 128
WIDTH = 64
FRAMES = 64
ROWS = 16
CELLS_ALL = 65536
GRS = 2
TEMPORAL_GROUPS = 5


def steps_of(own_key, shape, cuts, low, largest):
    def one(position, blocks):
        heights = jax.random.uniform(jax.random.fold_in(jax.random.fold_in(own_key, 6), position), (blocks,), jnp.float32, low / len(cuts), largest / len(cuts))
        return jnp.repeat(jnp.exp(heights), shape[position] // blocks).reshape((-1,) + (1,) * (len(shape) - position - 1))

    factor_of = one(*cuts[0])
    for cut in cuts[1:]:
        factor_of = factor_of * one(*cut)
    return factor_of


def centred(rng, extent, scale, reach, cuts=(), held_as=jnp.bfloat16):
    array = jax.random.normal(rng, extent, jnp.float32) * scale
    if len(cuts) > 0:
        array = steps_of(rng, extent, cuts, -0.22, 0.18) * array
    return jnp.clip(array, min=-reach, max=reach).astype(held_as)


def setup_inputs(seed: int = 0) -> dict:
    key_list = jax.random.split(jax.random.key(seed), 7)
    return {
        "output_first_half": centred(key_list[0], (FRAMES, ROWS, WIDTH, CH), 1.0, 6.0, ((0, 32), (1, 16))),
        "y_second": centred(key_list[1], (FRAMES, ROWS, WIDTH, CH), 1.0, 6.0, ((0, 32), (1, 16))),
        "cot_first": centred(key_list[2], (FRAMES, ROWS, WIDTH, CH), 1.0, 6.0, ((0, 32), (1, 16))),
        "cot_second": centred(key_list[3], (FRAMES, ROWS, WIDTH, CH), 1.0, 6.0, ((0, 32), (1, 16))),
        "weight_space": centred(key_list[4], (3, 3, GRS, GS, GS), (9 * GS) ** -0.5, 0.15625),
        "temporal_weight": centred(key_list[5], (3, TEMPORAL_GROUPS, GROUP_CHANNELS, GROUP_CHANNELS), (3 * GROUP_CHANNELS) ** -0.5, 0.3125),
    }


HAAR = 0.7071067811865476

def haar_pair_squeeze(input_frames):
    even_frames = input_frames[0::2].astype(jnp.float32)
    odd_frames = input_frames[1::2].astype(jnp.float32)
    return jnp.concatenate([(even_frames + odd_frames) * HAAR, (even_frames - odd_frames) * HAAR], axis=-1)

def unsqueeze_pairs(packed):
    half_ch = packed.shape[-1] // 2
    low_band = packed[..., :half_ch]
    high_band = packed[..., half_ch:]
    stacked = jnp.stack([(low_band + high_band) * HAAR, (low_band - high_band) * HAAR], axis=1)
    return stacked.reshape((2 * low_band.shape[0],) + low_band.shape[1:])

def silu_slope(values):
    sigmoid_v = jax.nn.sigmoid(values)
    return sigmoid_v * (1.0 + values * (1.0 - sigmoid_v))

def split_groups(tensor, groups):
    return tensor.reshape(tensor.shape[:-1] + (groups, tensor.shape[-1] // groups))

def merge_groups(tensor):
    return tensor.reshape(tensor.shape[:-2] + (tensor.shape[-2] * tensor.shape[-1],))

def time_apply(act_ext, temporal_weight):
    length = act_ext.shape[0] - 2
    groups = temporal_weight.shape[1]
    summed = None
    for offset in range(3):
        window = split_groups(act_ext[offset:offset + length].astype(jnp.float32), groups)
        partial_sum = jnp.einsum('t...gi,gio->t...go', window, temporal_weight[offset].astype(jnp.float32))
        summed = partial_sum if summed is None else summed + partial_sum
    return merge_groups(summed)

def time_back(cot_ext, temporal_weight):
    length = cot_ext.shape[0] - 2
    groups = temporal_weight.shape[1]
    summed = None
    for offset in range(3):
        window = split_groups(cot_ext[2 - offset:2 - offset + length].astype(jnp.float32), groups)
        partial_sum = jnp.einsum('t...go,gio->t...gi', window, temporal_weight[offset].astype(jnp.float32))
        summed = partial_sum if summed is None else summed + partial_sum
    return merge_groups(summed)

def time_wgrad(act_ext, cot_inner, groups):
    length = cot_inner.shape[0]
    cot_split = split_groups(cot_inner.astype(jnp.float32), groups)
    result = []
    for offset in range(3):
        window = split_groups(act_ext[offset:offset + length].astype(jnp.float32), groups)
        result.append(jnp.einsum('t...gi,t...go->gio', window, cot_split))
    return jnp.stack(result)

def time_core(y_ext, cot_ext, temporal_weight):
    squeezed = haar_pair_squeeze(y_ext)
    act_time = jax.nn.silu(squeezed).astype(jnp.bfloat16)
    temporal_cotangent = haar_pair_squeeze(cot_ext).astype(jnp.bfloat16)
    branch_time = unsqueeze_pairs(time_apply(act_time, temporal_weight)).astype(jnp.bfloat16)
    back_sum = time_back(temporal_cotangent, temporal_weight) * silu_slope(squeezed[1:-1])
    back_time = unsqueeze_pairs(back_sum).astype(jnp.bfloat16)
    sum_time = time_wgrad(act_time, temporal_cotangent[1:-1], temporal_weight.shape[1])
    return (branch_time, back_time, sum_time)

def space_apply(act_pad, weight_space):
    rows_in = act_pad.shape[-3] - 2
    cols_in = act_pad.shape[-2] - 2
    groups = weight_space.shape[2]
    summed = None
    for row_tap in range(3):
        for col_tap in range(3):
            window = act_pad[..., row_tap:row_tap + rows_in, col_tap:col_tap + cols_in, :]
            window = split_groups(window.astype(jnp.float32), groups)
            partial_sum = jnp.einsum('...gi,gio->...go', window, weight_space[row_tap, col_tap].astype(jnp.float32))
            summed = partial_sum if summed is None else summed + partial_sum
    return merge_groups(summed)

def space_back(cot_pad, weight_space):
    rows_in = cot_pad.shape[-3] - 2
    cols_in = cot_pad.shape[-2] - 2
    groups = weight_space.shape[2]
    summed = None
    for row_tap in range(3):
        for col_tap in range(3):
            window = cot_pad[..., 2 - row_tap:2 - row_tap + rows_in, 2 - col_tap:2 - col_tap + cols_in, :]
            window = split_groups(window.astype(jnp.float32), groups)
            partial_sum = jnp.einsum('...go,gio->...gi', window, weight_space[row_tap, col_tap].astype(jnp.float32))
            summed = partial_sum if summed is None else summed + partial_sum
    return merge_groups(summed)

def space_wgrad(act_pad, cot_inner, groups):
    rows_in = cot_inner.shape[-3]
    cols_in = cot_inner.shape[-2]
    cot_split = split_groups(cot_inner.astype(jnp.float32), groups)
    result = []
    for row_tap in range(3):
        row_list = []
        for col_tap in range(3):
            window = act_pad[..., row_tap:row_tap + rows_in, col_tap:col_tap + cols_in, :]
            window = split_groups(window.astype(jnp.float32), groups)
            row_list.append(jnp.einsum('...gi,...go->gio', window, cot_split))
        result.append(jnp.stack(row_list))
    return jnp.stack(result)

def reference(output_first_half, y_second, cot_first, cot_second, weight_space, temporal_weight):
    frame_pad = ((2, 2), (0, 0), (0, 0))

    def time_row(carry, inputs):
        row_y, row_cot = inputs
        branch_time, back_time, sum_time = time_core(jnp.pad(row_y, frame_pad), jnp.pad(row_cot, frame_pad), temporal_weight)
        return (carry + sum_time, (branch_time, back_time))
    init_time = jnp.zeros(temporal_weight.shape, jnp.float32)
    sum_time, (branch_rows, back_rows) = lax.scan(time_row, init_time, (jnp.swapaxes(output_first_half, 0, 1), jnp.swapaxes(cot_second, 0, 1)))
    branch_time = jnp.swapaxes(branch_rows, 0, 1)
    back_time = jnp.swapaxes(back_rows, 0, 1)
    space_pad = ((1, 1), (1, 1), (0, 0))

    def space_frame(carry, inputs):
        frame_y1, frame_y2, frame_c1, frame_c2, frame_branch, frame_back = inputs
        recovered = (frame_y2.astype(jnp.float32) - frame_branch.astype(jnp.float32)).astype(jnp.bfloat16)
        first_grad = (frame_c1.astype(jnp.float32) + frame_back.astype(jnp.float32)).astype(jnp.bfloat16)
        act_pad = jax.nn.silu(jnp.pad(recovered, space_pad).astype(jnp.float32)).astype(jnp.bfloat16)
        first_rec = (frame_y1.astype(jnp.float32) - space_apply(act_pad, weight_space)).astype(jnp.bfloat16)
        back_sum = space_back(jnp.pad(first_grad, space_pad), weight_space) * silu_slope(recovered.astype(jnp.float32))
        second_grad = (frame_c2.astype(jnp.float32) + back_sum).astype(jnp.bfloat16)
        return (carry + space_wgrad(act_pad, first_grad, weight_space.shape[2]), (first_rec, recovered, first_grad, second_grad))
    init_space = jnp.zeros(weight_space.shape, jnp.float32)
    sum_space, outs = lax.scan(space_frame, init_space, (output_first_half, y_second, cot_first, cot_second, branch_time, back_time))
    x_first, x_second, grad_first, grad_second = outs
    factor = 1.0 / math.sqrt(CELLS_ALL)
    return (x_first, x_second, grad_first, grad_second, sum_space.reshape(-1) * factor, sum_time.reshape(-1) * factor)
```

```python
import math

import jax
import jax.numpy as jnp
from jax import lax
from jax.experimental import pallas as pl
from jax.experimental.pallas import tpu as pltpu
from jax.sharding import PartitionSpec as P

HAAR = 0.7071067811865476
MESH = pl.DeviceIdType.MESH
F32, BF16 = jnp.float32, jnp.bfloat16


def place():
    tm, row = lax.axis_index("tm"), lax.axis_index("row")
    return tm // 4, tm % 4, row // 4, (row // 2) % 2, row % 2


def ident(z, yl, x, yh, c):
    return (z * 4 + yl, x * 4 + yh * 2 + c)


def greet(z, yl, x, yh, c):
    peers = []
    for dx in range(4):
        for h in range(2):
            for dc in range(2):
                if dx or h or dc:
                    peers.append(ident(z, yl, (x + dx) % 4, (yh + h) % 2, (c + dc) % 2))
    for j in range(1, 4):
        for h in range(2):
            peers.append(ident(z, (yl + j) % 4, x, (yh + h) % 2, c))
    for d in range(1, 8):
        peers.append(ident((z + d) % 8, yl, x, yh, c))
    barrier = pltpu.get_barrier_semaphore()
    for peer in peers:
        pl.semaphore_signal(barrier, inc=1, device_id=peer, device_id_type=MESH)
    pl.semaphore_wait(barrier, len(peers))


def sum_kernel(p, out, r0, s0, r1, s1, r2, s2, r3, fin, q_snd, q_rcv, x_snd, x_rcv, y_snd, y_rcv, z_snd, z_rcv, g_snd, g_rcv):
    z, yl, x, yh, c = place()
    greet(z, yl, x, yh, c)

    def send(src, dst, snd, rcv, peer):
        return pltpu.make_async_remote_copy(src_ref=src, dst_ref=dst, send_sem=snd, recv_sem=rcv, device_id=peer, device_id_type=MESH)

    started = []
    first = []
    for k in (1, 2, 3, 0):
        xp = (x + k) % 4
        copy = send(p.at[1 - c, xp], r0.at[xp], q_snd.at[k], q_rcv.at[k], ident(z, yl, x, yh, 1 - c))
        copy.start()
        first.append(copy)
    second = {}
    for n, k in enumerate((1, 2, 3, 0)):
        xp = (x + k) % 4
        first[n].wait_recv()
        for j in (1, 2, 3, 0):
            yp = (yl + j) % 4
            s0[xp, yp] = (p[c, xp, yp].astype(F32) + r0[xp, yp].astype(F32)).astype(BF16)
            if k:
                copy = send(s0.at[xp, yp], r1.at[k - 1, yp], x_snd.at[k - 1, j], x_rcv.at[k - 1, j], ident(z, yl, xp, yh, c))
                copy.start()
                second[k, j] = copy
    third = {}
    for j in (1, 2, 3, 0):
        yp = (yl + j) % 4
        for k in (1, 2, 3):
            second[k, j].wait_recv()
        total = s0[x, yp].astype(F32)
        for k in (1, 2, 3):
            total += r1[k - 1, yp].astype(F32)
        s1[yp] = total.astype(BF16)
        for h in (1, 0):
            if j or h:
                hp = (yh + h) % 2
                copy = send(s1.at[yp, pl.ds(hp * 4, 4)], r2.at[2 * j + h], y_snd.at[2 * j + h], y_rcv.at[2 * j + h], ident(z, yp, x, hp, c))
                copy.start()
                third[j, h] = copy
    total = s1[yl, pl.ds(yh * 4, 4)].astype(F32)
    for j, h in third:
        third[j, h].wait_recv()
    for j, h in third:
        total += r2[2 * j + h].astype(F32)
    s2[...] = total.astype(BF16)
    mine = z // 4 == yh
    for d in range(1, 8):
        zp = (z + d) % 8

        @pl.when(zp // 4 == yh)
        def _():
            send(s2.at[zp % 4], r3.at[d - 1], z_snd.at[d - 1], z_rcv.at[d - 1], ident(zp, yl, x, yh, c)).start()

    @pl.when(mine)
    def _():
        for d in range(1, 8):
            send(s2.at[0], r3.at[d - 1], z_snd.at[d - 1], z_rcv.at[d - 1], ident((z + d) % 8, yl, x, yh, c)).wait_recv()
        last = s2[z % 4].astype(F32)
        for d in range(1, 8):
            last += r3[d - 1].astype(F32)
        fin[c * 4 + x] = last
        for dx in range(4):
            for h in range(2):
                for dc in range(2):
                    if dx or h or dc:
                        n = dx * 2 + dc
                        send(fin.at[c * 4 + x], fin.at[c * 4 + x], g_snd.at[n, h], g_rcv.at[n], ident(z, yl, (x + dx) % 4, (yh + h) % 2, (c + dc) % 2)).start()

    for dx in range(4):
        for dc in range(2):
            n = dx * 2 + dc
            src = ((c + dc) % 2) * 4 + (x - dx) % 4

            def wait():
                send(fin.at[src], fin.at[src], g_snd.at[n, 0], g_rcv.at[n], ident(z, yl, (x + dx) % 4, yh, (c + dc) % 2)).wait_recv()

            if n:
                wait()
            else:
                pl.when(jnp.logical_not(mine))(lambda: send(fin.at[src], fin.at[src], g_snd.at[0, 1], g_rcv.at[0], ident(z, yl, x, 1 - yh, c)).wait_recv())
    out[...] = fin[...]
    for copy in first + list(second.values()) + list(third.values()):
        copy.wait_send()
    for d in range(1, 8):
        zp = (z + d) % 8

        @pl.when(zp // 4 == yh)
        def _():
            send(s2.at[zp % 4], r3.at[d - 1], z_snd.at[d - 1], z_rcv.at[d - 1], ident(zp, yl, x, yh, c)).wait_send()

    @pl.when(mine)
    def _():
        for dx in range(4):
            for h in range(2):
                for dc in range(2):
                    if dx or h or dc:
                        n = dx * 2 + dc
                        send(fin.at[c * 4 + x], fin.at[c * 4 + x], g_snd.at[n, h], g_rcv.at[n], ident(z, yl, (x + dx) % 4, (yh + h) % 2, (c + dc) % 2)).wait_send()


def summed(p):
    dma = pltpu.SemaphoreType.DMA
    out = pl.pallas_call(
        sum_kernel,
        out_shape=jax.ShapeDtypeStruct((8, 3, 8, 128), F32),
        in_specs=[pl.BlockSpec(memory_space=pltpu.VMEM)],
        out_specs=pl.BlockSpec(memory_space=pltpu.VMEM),
        scratch_shapes=[
            pltpu.VMEM((4, 4, 8, 3, 8, 128), BF16),
            pltpu.VMEM((4, 4, 8, 3, 8, 128), BF16),
            pltpu.VMEM((3, 4, 8, 3, 8, 128), BF16),
            pltpu.VMEM((4, 8, 3, 8, 128), BF16),
            pltpu.VMEM((8, 4, 3, 8, 128), BF16),
            pltpu.VMEM((4, 3, 8, 128), BF16),
            pltpu.VMEM((7, 3, 8, 128), BF16),
            pltpu.VMEM((8, 3, 8, 128), F32),
            dma((4,)), dma((4,)), dma((3, 4)), dma((3, 4)), dma((8,)), dma((8,)), dma((7,)), dma((7,)), dma((8, 2)), dma((8,)),
        ],
        compiler_params=pltpu.CompilerParams(collective_id=3, has_side_effects=True),
        name="sum_terms",
    )(p)
    return out.reshape(192, 128)


def packed(sum_space, sum_time):
    s = sum_space.reshape(32, 90, 160)
    s = jnp.pad(s, ((0, 0), (0, 6), (0, 0)))
    rest = s[:, :, 128:].reshape(32, 4, 24, 32).transpose(0, 2, 1, 3).reshape(32, 24, 128)
    t = jnp.pad(sum_time.reshape(32, 60, 128), ((0, 0), (0, 12), (0, 0)))
    p = jnp.concatenate([s[:, :, :128], rest, t], axis=1).astype(BF16)
    return p.reshape(8, 4, 2, 4, 3, 8, 128).transpose(2, 3, 1, 0, 4, 5, 6)


def shares(chunk, row):
    rest = chunk[96:120].reshape(24, 4, 32).transpose(1, 0, 2).reshape(96, 32)
    space = jnp.concatenate([chunk[:90], rest[:90]], axis=1).reshape(-1)
    time = chunk[120:180].reshape(-1)
    return lax.dynamic_slice(space, (900 * row,), (900,)), lax.dynamic_slice(time, (480 * row,), (480,))


def extended(x, sides, width):
    for axis, dim in sides:
        peers, length = (lax.axis_size(axis), x.shape[dim])
        up = [(i, (i + 1) % peers) for i in range(peers - 1)]
        down = [(j, i) for i, j in up]
        last = lax.slice_in_dim(x, length - width, length, axis=dim)
        initial = lax.slice_in_dim(x, 0, width, axis=dim)
        before = lax.ppermute(last, axis, up)
        after = lax.ppermute(initial, axis, down)
        x = jnp.concatenate([before, x, after], axis=dim)
    return x


def haar_pair_squeeze(input_frames):
    even_frames = input_frames[0::2].astype(jnp.float32)
    odd_frames = input_frames[1::2].astype(jnp.float32)
    return jnp.concatenate(
        [(even_frames + odd_frames) * HAAR, (even_frames - odd_frames) * HAAR], axis=-1
    )


def unsqueeze_pairs(packed):
    half_ch = packed.shape[-1] // 2
    low_band = packed[..., :half_ch]
    high_band = packed[..., half_ch:]
    stacked = jnp.stack([(low_band + high_band) * HAAR, (low_band - high_band) * HAAR], axis=1)
    return stacked.reshape((2 * low_band.shape[0],) + low_band.shape[1:])


def silu_slope(values):
    sigmoid_v = jax.nn.sigmoid(values)
    return sigmoid_v * (1.0 + values * (1.0 - sigmoid_v))


def split_groups(tensor, groups):
    return tensor.reshape(tensor.shape[:-1] + (groups, tensor.shape[-1] // groups))


def merge_groups(tensor):
    return tensor.reshape(tensor.shape[:-2] + (tensor.shape[-2] * tensor.shape[-1],))


def time_apply(act_ext, temporal_weight):
    length = act_ext.shape[0] - 2
    groups = temporal_weight.shape[1]
    summed = None
    for offset in range(3):
        window = split_groups(act_ext[offset : offset + length], groups)
        partial_sum = jnp.einsum(
            "t...gi,gio->t...go",
            window,
            temporal_weight[offset],
            preferred_element_type=jnp.float32,
        )
        summed = partial_sum if summed is None else summed + partial_sum
    return merge_groups(summed)


def time_back(cot_ext, temporal_weight):
    length = cot_ext.shape[0] - 2
    groups = temporal_weight.shape[1]
    summed = None
    for offset in range(3):
        window = split_groups(cot_ext[2 - offset : 2 - offset + length], groups)
        partial_sum = jnp.einsum(
            "t...go,gio->t...gi",
            window,
            temporal_weight[offset],
            preferred_element_type=jnp.float32,
        )
        summed = partial_sum if summed is None else summed + partial_sum
    return merge_groups(summed)


def time_wgrad(act_ext, cot_inner, groups):
    length = cot_inner.shape[0]
    cot_split = split_groups(cot_inner, groups)
    result = []
    for offset in range(3):
        window = split_groups(act_ext[offset : offset + length], groups)
        result.append(
            jnp.einsum("t...gi,t...go->gio", window, cot_split, preferred_element_type=jnp.float32)
        )
    return jnp.stack(result)


def time_core(y_ext, cot_ext, temporal_weight):
    squeezed = haar_pair_squeeze(y_ext)
    act_time = jax.nn.silu(squeezed).astype(jnp.bfloat16)
    temporal_cotangent = haar_pair_squeeze(cot_ext).astype(jnp.bfloat16)
    branch_time = unsqueeze_pairs(time_apply(act_time, temporal_weight)).astype(jnp.bfloat16)
    back_sum = time_back(temporal_cotangent, temporal_weight) * silu_slope(squeezed[1:-1])
    back_time = unsqueeze_pairs(back_sum).astype(jnp.bfloat16)
    sum_time = time_wgrad(act_time, temporal_cotangent[1:-1], temporal_weight.shape[1])
    return (branch_time, back_time, sum_time)


def space_apply(act_pad, weight_space):
    rows_in = act_pad.shape[-3] - 2
    cols_in = act_pad.shape[-2] - 2
    groups = weight_space.shape[2]
    summed = None
    for row_tap in range(3):
        for col_tap in range(3):
            window = split_groups(
                act_pad[..., row_tap : row_tap + rows_in, col_tap : col_tap + cols_in, :], groups
            )
            partial_sum = jnp.einsum(
                "...gi,gio->...go",
                window,
                weight_space[row_tap, col_tap],
                preferred_element_type=jnp.float32,
            )
            summed = partial_sum if summed is None else summed + partial_sum
    return merge_groups(summed)


def space_back(cot_pad, weight_space):
    rows_in = cot_pad.shape[-3] - 2
    cols_in = cot_pad.shape[-2] - 2
    groups = weight_space.shape[2]
    summed = None
    for row_tap in range(3):
        for col_tap in range(3):
            window = cot_pad[
                ..., 2 - row_tap : 2 - row_tap + rows_in, 2 - col_tap : 2 - col_tap + cols_in, :
            ]
            window = split_groups(window, groups)
            partial_sum = jnp.einsum(
                "...go,gio->...gi",
                window,
                weight_space[row_tap, col_tap],
                preferred_element_type=jnp.float32,
            )
            summed = partial_sum if summed is None else summed + partial_sum
    return merge_groups(summed)


def space_wgrad(act_pad, cot_inner, groups):
    rows_in = cot_inner.shape[-3]
    cols_in = cot_inner.shape[-2]
    cot_split = split_groups(cot_inner, groups)
    result = []
    for row_tap in range(3):
        row_list = []
        for col_tap in range(3):
            window = split_groups(
                act_pad[..., row_tap : row_tap + rows_in, col_tap : col_tap + cols_in, :], groups
            )
            row_list.append(
                jnp.einsum(
                    "...gi,...go->gio", window, cot_split, preferred_element_type=jnp.float32
                )
            )
        result.append(jnp.stack(row_list))
    return jnp.stack(result)


def per_device(output_first_half, y_second, cot_first, cot_second, weight_space, temporal_weight):
    joined = jnp.stack([output_first_half, cot_second])
    rimmed = extended(joined, (("tm", 1),), 2)
    branch_time, back_time, sum_time = time_core(rimmed[0], rimmed[1], temporal_weight)
    cells_all = (
        output_first_half.shape[0]
        * output_first_half.shape[1]
        * output_first_half.shape[2]
        * lax.axis_size("tm")
        * lax.axis_size("row")
    )
    factor = 1.0 / math.sqrt(cells_all)
    recovered = (y_second.astype(jnp.float32) - branch_time.astype(jnp.float32)).astype(
        jnp.bfloat16
    )
    first_grad = (cot_first.astype(jnp.float32) + back_time.astype(jnp.float32)).astype(
        jnp.bfloat16
    )
    stacked = jnp.stack([recovered, first_grad])
    row_ext = extended(stacked, (("row", 2),), 1)
    col_pad = ((0, 0), (0, 0), (1, 1), (0, 0))
    act_pad = jax.nn.silu(jnp.pad(row_ext[0], col_pad).astype(jnp.float32)).astype(jnp.bfloat16)
    cot_pad = jnp.pad(row_ext[1], col_pad)
    first_rec = (output_first_half.astype(jnp.float32) - space_apply(act_pad, weight_space)).astype(
        jnp.bfloat16
    )
    back_sum = space_back(cot_pad, weight_space) * silu_slope(recovered.astype(jnp.float32))
    second_grad = (cot_second.astype(jnp.float32) + back_sum).astype(jnp.bfloat16)
    sum_space = space_wgrad(act_pad, first_grad, weight_space.shape[2])
    chunk = summed(packed(sum_space, sum_time))
    space_share, time_share = shares(chunk, lax.axis_index("row"))
    return (
        first_rec,
        recovered,
        first_grad,
        second_grad,
        space_share * factor,
        time_share * factor,
    )


def solution(mesh):
    in_specs = (
        P("tm", "row", None, None),
        P("tm", "row", None, None),
        P("tm", "row", None, None),
        P("tm", "row", None, None),
        P(),
        P(),
    )
    out_specs = (
        P("tm", "row", None, None),
        P("tm", "row", None, None),
        P("tm", "row", None, None),
        P("tm", "row", None, None),
        P(("tm", "row")),
        P(("tm", "row")),
    )
    return jax.shard_map(
        per_device, mesh=mesh, in_specs=in_specs, out_specs=out_specs, check_vma=False
    )
```

```python
import math

import jax
import jax.numpy as jnp
from jax import lax
from jax.experimental import pallas as pl
from jax.experimental.pallas import tpu as pltpu
from jax.sharding import PartitionSpec as P

MESH = pl.DeviceIdType.MESH
F32, BF16 = jnp.float32, jnp.bfloat16
HAAR = 0.7071067811865476


def place():
    tm, row = lax.axis_index("tm"), lax.axis_index("row")
    return tm // 4, tm % 4, row // 4, (row // 2) % 2, row % 2


def ident(z, yl, x, yh, c):
    return (z * 4 + yl, x * 4 + yh * 2 + c)


def greet(z, yl, x, yh, c):
    peers = []
    for dx in range(4):
        for h in range(2):
            for dc in range(2):
                if dx or h or dc:
                    peers.append(ident(z, yl, (x + dx) % 4, (yh + h) % 2, (c + dc) % 2))
    for j in range(1, 4):
        for h in range(2):
            peers.append(ident(z, (yl + j) % 4, x, (yh + h) % 2, c))
    for d in range(1, 8):
        peers.append(ident((z + d) % 8, yl, x, yh, c))
    barrier = pltpu.get_barrier_semaphore()
    for peer in peers:
        pl.semaphore_signal(barrier, inc=1, device_id=peer, device_id_type=MESH)
    pl.semaphore_wait(barrier, len(peers))


def sum_kernel(p, out, r0, s0, r1, s1, r2, s2, r3, fin, q_snd, q_rcv, x_snd, x_rcv, y_snd, y_rcv, z_snd, z_rcv, g_snd, g_rcv):
    z, yl, x, yh, c = place()
    greet(z, yl, x, yh, c)

    def send(src, dst, snd, rcv, peer):
        return pltpu.make_async_remote_copy(src_ref=src, dst_ref=dst, send_sem=snd, recv_sem=rcv, device_id=peer, device_id_type=MESH)

    started = []
    first = []
    for k in (1, 2, 3, 0):
        xp = (x + k) % 4
        copy = send(p.at[1 - c, xp], r0.at[xp], q_snd.at[k], q_rcv.at[k], ident(z, yl, x, yh, 1 - c))
        copy.start()
        first.append(copy)
    second = {}
    for n, k in enumerate((1, 2, 3, 0)):
        xp = (x + k) % 4
        first[n].wait_recv()
        for j in (1, 2, 3, 0):
            yp = (yl + j) % 4
            s0[xp, yp] = (p[c, xp, yp].astype(F32) + r0[xp, yp].astype(F32)).astype(BF16)
            if k:
                copy = send(s0.at[xp, yp], r1.at[k - 1, yp], x_snd.at[k - 1, j], x_rcv.at[k - 1, j], ident(z, yl, xp, yh, c))
                copy.start()
                second[k, j] = copy
    third = {}
    for j in (1, 2, 3, 0):
        yp = (yl + j) % 4
        for k in (1, 2, 3):
            second[k, j].wait_recv()
        total = s0[x, yp].astype(F32)
        for k in (1, 2, 3):
            total += r1[k - 1, yp].astype(F32)
        s1[yp] = total.astype(BF16)
        for h in (1, 0):
            if j or h:
                hp = (yh + h) % 2
                copy = send(s1.at[yp, pl.ds(hp * 4, 4)], r2.at[2 * j + h], y_snd.at[2 * j + h], y_rcv.at[2 * j + h], ident(z, yp, x, hp, c))
                copy.start()
                third[j, h] = copy
    total = s1[yl, pl.ds(yh * 4, 4)].astype(F32)
    for j, h in third:
        third[j, h].wait_recv()
    for j, h in third:
        total += r2[2 * j + h].astype(F32)
    s2[...] = total.astype(BF16)
    mine = z // 4 == yh
    for d in range(1, 8):
        zp = (z + d) % 8

        @pl.when(zp // 4 == yh)
        def _():
            send(s2.at[zp % 4], r3.at[d - 1], z_snd.at[d - 1], z_rcv.at[d - 1], ident(zp, yl, x, yh, c)).start()

    @pl.when(mine)
    def _():
        for d in range(1, 8):
            send(s2.at[0], r3.at[d - 1], z_snd.at[d - 1], z_rcv.at[d - 1], ident((z + d) % 8, yl, x, yh, c)).wait_recv()
        last = s2[z % 4].astype(F32)
        for d in range(1, 8):
            last += r3[d - 1].astype(F32)
        fin[c * 4 + x] = last
        for dx in range(4):
            for h in range(2):
                for dc in range(2):
                    if dx or h or dc:
                        n = dx * 2 + dc
                        send(fin.at[c * 4 + x], fin.at[c * 4 + x], g_snd.at[n, h], g_rcv.at[n], ident(z, yl, (x + dx) % 4, (yh + h) % 2, (c + dc) % 2)).start()

    for dx in range(4):
        for dc in range(2):
            n = dx * 2 + dc
            src = ((c + dc) % 2) * 4 + (x - dx) % 4

            def wait():
                send(fin.at[src], fin.at[src], g_snd.at[n, 0], g_rcv.at[n], ident(z, yl, (x + dx) % 4, yh, (c + dc) % 2)).wait_recv()

            if n:
                wait()
            else:
                pl.when(jnp.logical_not(mine))(lambda: send(fin.at[src], fin.at[src], g_snd.at[0, 1], g_rcv.at[0], ident(z, yl, x, 1 - yh, c)).wait_recv())
    out[...] = fin[...]
    for copy in first + list(second.values()) + list(third.values()):
        copy.wait_send()
    for d in range(1, 8):
        zp = (z + d) % 8

        @pl.when(zp // 4 == yh)
        def _():
            send(s2.at[zp % 4], r3.at[d - 1], z_snd.at[d - 1], z_rcv.at[d - 1], ident(zp, yl, x, yh, c)).wait_send()

    @pl.when(mine)
    def _():
        for dx in range(4):
            for h in range(2):
                for dc in range(2):
                    if dx or h or dc:
                        n = dx * 2 + dc
                        send(fin.at[c * 4 + x], fin.at[c * 4 + x], g_snd.at[n, h], g_rcv.at[n], ident(z, yl, (x + dx) % 4, (yh + h) % 2, (c + dc) % 2)).wait_send()


def summed(p):
    dma = pltpu.SemaphoreType.DMA
    out = pl.pallas_call(
        sum_kernel,
        out_shape=jax.ShapeDtypeStruct((8, 3, 8, 128), F32),
        in_specs=[pl.BlockSpec(memory_space=pltpu.VMEM)],
        out_specs=pl.BlockSpec(memory_space=pltpu.VMEM),
        scratch_shapes=[
            pltpu.VMEM((4, 4, 8, 3, 8, 128), BF16),
            pltpu.VMEM((4, 4, 8, 3, 8, 128), BF16),
            pltpu.VMEM((3, 4, 8, 3, 8, 128), BF16),
            pltpu.VMEM((4, 8, 3, 8, 128), BF16),
            pltpu.VMEM((8, 4, 3, 8, 128), BF16),
            pltpu.VMEM((4, 3, 8, 128), BF16),
            pltpu.VMEM((7, 3, 8, 128), BF16),
            pltpu.VMEM((8, 3, 8, 128), F32),
            dma((4,)), dma((4,)), dma((3, 4)), dma((3, 4)), dma((8,)), dma((8,)), dma((7,)), dma((7,)), dma((8, 2)), dma((8,)),
        ],
        compiler_params=pltpu.CompilerParams(collective_id=3, has_side_effects=True),
        name="sum_terms",
    )(p)
    return out.reshape(192, 128)


def sigmoid(v):
    return 1.0 / (1.0 + jnp.exp(-v))


def slope(v):
    s = sigmoid(v)
    return s * (1.0 + v * (1.0 - s))


def dot(a, b, ca, cb):
    return lax.dot_general(a, b, (((ca,), (cb,)), ((), ())), preferred_element_type=F32)


def block_kernel(y1, y2, c1, c2, ws, wt, xf, xs, gf, gs, p, tb, hb, sq, cs, wide, pa, pg, sa, rq, g, gt, t_snd, t_rcv, r_snd, r_rcv):
    tm, row = lax.axis_index("tm"), lax.axis_index("row")
    barrier = pltpu.get_barrier_semaphore()
    for peer in (((tm + 1) % 32, row), ((tm + 31) % 32, row), (tm, (row + 1) % 16), (tm, (row + 15) % 16)):
        pl.semaphore_signal(barrier, inc=1, device_id=peer, device_id_type=MESH)

    for n, ref in enumerate((y1, c2)):
        even, odd = ref[0].astype(F32), ref[1].astype(F32)
        sq[n, :, 0:320] = (even + odd) * HAAR
        sq[n, :, 320:640] = (even - odd) * HAAR
    v = sq[0]
    tb[1, 0] = (v * sigmoid(v)).astype(BF16)
    tb[1, 1] = sq[1].astype(BF16)
    zero_t = jnp.zeros((2, 64, 640), BF16)
    zero_r = jnp.zeros((2, 128, 320), BF16)
    first_t, last_t, first_r, last_r = tm == 0, tm == 31, row == 0, row == 15

    def clear(where, ref, slot, zero):
        @pl.when(where)
        def _():
            ref[slot] = zero

    clear(first_t, tb, 0, zero_t)
    clear(last_t, tb, 2, zero_t)
    clear(first_r, hb, 0, zero_r)
    clear(last_r, hb, 2, zero_r)
    pad = jnp.zeros((3, 2, 2, 8, 160), F32)
    for ref in (pa, pg):
        ref[:, :, :, 0:8] = pad
        ref[:, :, :, 72:80] = pad

    pl.semaphore_wait(barrier, 4)

    def swap(ref, snd, rcv, up, down, first, last):
        ahead = pltpu.make_async_remote_copy(src_ref=ref.at[1], dst_ref=ref.at[0], send_sem=snd.at[0], recv_sem=rcv.at[0], device_id=up, device_id_type=MESH)
        behind = pltpu.make_async_remote_copy(src_ref=ref.at[1], dst_ref=ref.at[2], send_sem=snd.at[1], recv_sem=rcv.at[1], device_id=down, device_id_type=MESH)
        has_ahead, has_behind = jnp.logical_not(last), jnp.logical_not(first)

        def start():
            pl.when(has_ahead)(ahead.start)
            pl.when(has_behind)(behind.start)

        def arrive():
            pl.when(has_behind)(ahead.wait_recv)
            pl.when(has_ahead)(behind.wait_recv)

        def sent():
            pl.when(has_ahead)(ahead.wait_send)
            pl.when(has_behind)(behind.wait_send)

        return start, arrive, sent

    t_start, t_arrive, t_sent = swap(tb, t_snd, t_rcv, ((tm + 1) % 32, row), ((tm + 31) % 32, row), first_t, last_t)
    r_start, r_arrive, r_sent = swap(hb, r_snd, r_rcv, (tm, (row + 1) % 16), (tm, (row + 15) % 16), first_r, last_r)
    t_start()

    def time_taps(ks):
        for q in range(5):
            at = pl.ds(q * 128, 128)
            ahead, back = None, None
            for k in ks:
                one = dot(tb[k, 0, :, at], wt[k, q], 1, 0)
                two = dot(tb[2 - k, 1, :, at], wt[k, q], 1, 1)
                ahead, back = (one, two) if ahead is None else (ahead + one, back + two)
            yield at, ahead, back

    def time_terms(ks):
        for k in ks:
            for q in range(5):
                at = pl.ds(q * 128, 128)
                gt[pl.ds((k * 5 + q) * 16, 16)] = dot(tb[1, 0, :, at], tb[2 - k, 1, :, at], 0, 0).reshape(16, 8, 128)

    for at, ahead, back in time_taps((1,)):
        cs[0, :, at] = ahead
        cs[1, :, at] = back
    time_terms((1,))
    t_arrive()
    for at, ahead, back in time_taps((0, 2)):
        cs[0, :, at] = cs[0, :, at] + ahead
        cs[1, :, at] = (cs[1, :, at] + back) * slope(sq[0, :, at])
    for n, (src, out) in enumerate(((y2, xs), (c1, gf))):
        low, high = cs[n, :, 0:320], cs[n, :, 320:640]
        for f in range(2):
            part = ((low + high if f == 0 else low - high) * HAAR).astype(BF16).astype(F32)
            new = (src[f].astype(F32) - part if n == 0 else src[f].astype(F32) + part).astype(BF16)
            out[f] = new
            held = new
            if n == 0:
                w = new.astype(F32)
                held = (w * sigmoid(w)).astype(BF16)
            hb[1, n, pl.ds(f * 64, 64)] = held
    r_start()
    time_terms((0, 2))

    def spread(slot):
        for n, ref in enumerate((pa, pg)):
            wide[n] = hb[slot, n].astype(F32)
            for q in range(2):
                ref[slot, q, :, 8:72] = wide[n, :, pl.ds(q * 160, 160)].reshape(2, 64, 160)

    spread(1)
    for q in range(2):
        rq[q, :, 0:128] = wide[1, :, pl.ds(q * 160, 128)]
        for n in range(4):
            rq[q, :, pl.ds(128 + 32 * n, 32)] = wide[1, :, pl.ds(q * 160 + 128, 32)]

    def space_terms(rows):
        for q in range(2):
            right = rq[q].astype(BF16)
            for a in rows:
                for b in range(3):
                    tap = a * 3 + b
                    left = pa[a, q, :, pl.ds(7 + b, 64)].reshape(128, 160).astype(BF16)
                    sa[tap, q] = left
                    g[pl.ds((tap * 2 + q) * 20, 20)] = dot(left, right, 0, 0).reshape(20, 8, 256)

    def space_taps(rows, q):
        ahead, back = None, None
        for a in rows:
            for b in range(3):
                one = dot(sa[a * 3 + b, q], ws[a, b, q], 1, 0)
                moved = pg[2 - a, q, :, pl.ds(9 - b, 64)].reshape(128, 160).astype(BF16)
                two = dot(moved, ws[a, b, q], 1, 1)
                ahead, back = (one, two) if ahead is None else (ahead + one, back + two)
        return ahead, back

    space_terms((1,))
    r_arrive()
    spread(0)
    spread(2)
    space_terms((0, 2))
    lane = lax.broadcasted_iota(jnp.int32, (3, 8, 128), 2)

    def pack(chunk, carry):
        z, yl = chunk // 4, chunk % 4
        tiles = g[pl.ds((45 * chunk) // 4, 12)]
        for n in range(4):
            p[0, n, yl, z] = tiles[3 * n : 3 * n + 3, :, 0:128].astype(BF16)
        rest = tiles[:, :, 128:256]
        rest = jnp.where(lane < 32, rest[0:3], jnp.where(lane < 64, rest[3:6], jnp.where(lane < 96, rest[6:9], rest[9:12])))
        p[1, 0, yl, z] = rest.astype(BF16)
        tiles = gt[pl.ds((15 * chunk) // 2, 8)]
        p[1, 1, yl, z] = tiles[0:3].astype(BF16)
        p[1, 2, yl, z] = tiles[3:6].astype(BF16)
        p[1, 3, yl, z, 0:2] = tiles[6:8].astype(BF16)
        p[1, 3, yl, z, 2:3] = jnp.zeros((1, 8, 128), BF16)
        return carry

    lax.fori_loop(0, 32, pack, 0)
    for q in range(2):
        ahead, back = space_taps((0, 1, 2), q)
        wide[0, :, pl.ds(q * 160, 160)] = ahead
        wide[1, :, pl.ds(q * 160, 160)] = back
    for f in range(2):
        at = pl.ds(f * 64, 64)
        xf[f] = (y1[f].astype(F32) - wide[0, at]).astype(BF16)
        gs[f] = (c2[f].astype(F32) + wide[1, at] * slope(xs[f].astype(F32))).astype(BF16)
    t_sent()
    r_sent()


def block(y1, y2, c1, c2, ws, wt):
    dma = pltpu.SemaphoreType.DMA
    here = pl.BlockSpec(memory_space=pltpu.VMEM)
    one = jax.ShapeDtypeStruct((2, 64, 320), BF16)
    return pl.pallas_call(
        block_kernel,
        out_shape=[one] * 4 + [jax.ShapeDtypeStruct((2, 4, 4, 8, 3, 8, 128), BF16)],
        in_specs=[here] * 6,
        out_specs=[here] * 5,
        scratch_shapes=[
            pltpu.VMEM((3, 2, 64, 640), BF16),
            pltpu.VMEM((3, 2, 128, 320), BF16),
            pltpu.VMEM((2, 64, 640), F32),
            pltpu.VMEM((2, 64, 640), F32),
            pltpu.VMEM((2, 128, 320), F32),
            pltpu.VMEM((3, 2, 2, 80, 160), F32),
            pltpu.VMEM((3, 2, 2, 80, 160), F32),
            pltpu.VMEM((9, 2, 128, 160), BF16),
            pltpu.VMEM((2, 128, 256), F32),
            pltpu.VMEM((360, 8, 256), F32),
            pltpu.VMEM((240, 8, 128), F32),
            dma((2,)), dma((2,)), dma((2,)), dma((2,)),
        ],
        compiler_params=pltpu.CompilerParams(collective_id=5, has_side_effects=True, vmem_limit_bytes=40 * 1024 * 1024),
        name="block",
    )(y1, y2, c1, c2, ws, wt)


def shares(chunk, tm, row):
    rest = chunk[96:120].reshape(24, 4, 32).transpose(1, 0, 2).reshape(96, 32)
    space = jnp.concatenate([chunk[:96], rest], axis=1).reshape(-1)
    time = chunk[120:184].reshape(-1)
    return (
        lax.dynamic_slice(space, (90 * tm % 8 * 160 + 900 * row,), (900,)),
        lax.dynamic_slice(time, (60 * tm % 8 * 128 + 480 * row,), (480,)),
    )


def per_device(output_first_half, y_second, cot_first, cot_second, weight_space, temporal_weight):
    cells_all = output_first_half.shape[0] * output_first_half.shape[1] * output_first_half.shape[2] * lax.axis_size("tm") * lax.axis_size("row")
    factor = 1.0 / math.sqrt(cells_all)
    flat = [v.reshape(2, 64, 320) for v in (output_first_half, y_second, cot_first, cot_second)]
    *outs, p = block(*flat, weight_space, temporal_weight)
    chunk = summed(p)
    space_share, time_share = shares(chunk, lax.axis_index("tm"), lax.axis_index("row"))
    return tuple(v.reshape(output_first_half.shape) for v in outs) + (space_share * factor, time_share * factor)


def solution(mesh):
    in_specs = (
        P("tm", "row", None, None),
        P("tm", "row", None, None),
        P("tm", "row", None, None),
        P("tm", "row", None, None),
        P(),
        P(),
    )
    out_specs = (
        P("tm", "row", None, None),
        P("tm", "row", None, None),
        P("tm", "row", None, None),
        P("tm", "row", None, None),
        P(("tm", "row")),
        P(("tm", "row")),
    )
    return jax.shard_map(
        per_device, mesh=mesh, in_specs=in_specs, out_specs=out_specs, check_vma=False
    )
```

```python
import math

import jax
import jax.numpy as jnp
from jax import lax
from jax.experimental import pallas as pl
from jax.experimental.pallas import tpu as pltpu
from jax.sharding import PartitionSpec as P

MESH = pl.DeviceIdType.MESH
F32, BF16 = jnp.float32, jnp.bfloat16
HAAR = 0.7071067811865476
SHIFT, EARLY = 5, 2


def place():
    tm, row = lax.axis_index("tm"), lax.axis_index("row")
    return tm // 4, tm % 4, row // 4, (row // 2) % 2, row % 2


def ident(z, yl, x, yh, c):
    return (z * 4 + yl, x * 4 + yh * 2 + c)


def sigmoid(v):
    return 1.0 / (1.0 + jnp.exp(-v))


def slope(v):
    s = sigmoid(v)
    return s * (1.0 + v * (1.0 - s))


def dot(a, b, ca, cb):
    return lax.dot_general(a, b, (((ca,), (cb,)), ((), ())), preferred_element_type=F32)


def send(src, dst, snd, rcv, peer):
    return pltpu.make_async_remote_copy(
        src_ref=src, dst_ref=dst, send_sem=snd, recv_sem=rcv, device_id=peer, device_id_type=MESH
    )


def greet(z, yl, x, yh, c):
    tm, row = z * 4 + yl, x * 4 + yh * 2 + c
    peers = [((tm + 1) % 32, row), ((tm + 31) % 32, row), (tm, (row + 2 * c + 15) % 16)]
    for dx in range(4):
        for h in range(2):
            for dc in range(2):
                if dx or h or dc:
                    peers.append(ident(z, yl, (x + dx) % 4, (yh + h) % 2, (c + dc) % 2))
    for j in range(1, 4):
        for h in range(2):
            peers.append(ident(z, (yl + j) % 4, x, (yh + h) % 2, c))
    for d in range(1, 8):
        peers.append(ident((z + d) % 8, yl, x, yh, c))
    barrier = pltpu.get_barrier_semaphore()
    for peer in peers:
        pl.semaphore_signal(barrier, inc=1, device_id=peer, device_id_type=MESH)
    return barrier, len(peers)


def block_kernel(
    y1h, y2h, c1h, c2h, wsh, wth, xf, xs, gf, gs, out,
    y1, y2, c1, c2, ws, wt, tb, hb, sq, cs, wide, pa, pg, sa, rq, g, gt, rt, s0, r1, s1, r2, s2, r3, fin,
    in_sem, t_snd, t_rcv, n_snd, n_rcv, r_snd, r_rcv, f_snd, f_rcv, q_snd, q_rcv, x_snd, x_rcv, y_snd, y_rcv, z_snd, z_rcv, g_snd, g_rcv,
):
    z, yl, x, yh, c = place()
    tm, row = z * 4 + yl, x * 4 + yh * 2 + c
    loads = [
        pltpu.make_async_copy(src, dst, in_sem.at[n])
        for n, (src, dst) in enumerate(((y1h, y1), (c2h, c2), (wth, wt), (y2h, y2), (c1h, c1), (wsh, ws)))
    ]
    for load in loads:
        load.start()
    barrier, met = greet(z, yl, x, yh, c)
    partner = ident(z, yl, x, yh, 1 - c)
    first_t, last_t = tm == 0, tm == 31
    own, other, far = 1 + c, 2 - c, 3 * c
    has_far = jnp.logical_not(jnp.logical_or(row == 0, row == 15))
    pad = jnp.zeros((4, 2, 2, 8, 160), F32)
    for ref in (pa, pg):
        ref[:, :, :, 0:8] = pad
        ref[:, :, :, 72:80] = pad

    @pl.when(first_t)
    def _():
        tb[0] = jnp.zeros((2, 64, 640), BF16)

    @pl.when(last_t)
    def _():
        tb[2] = jnp.zeros((2, 64, 640), BF16)

    @pl.when(jnp.logical_not(has_far))
    def _():
        hb[far] = jnp.zeros((2, 128, 320), BF16)

    for n, ref in enumerate((y1, c2)):
        loads[n].wait()
        even, odd = ref[0].astype(F32), ref[1].astype(F32)
        sq[n, :, 0:320] = (even + odd) * HAAR
        sq[n, :, 320:640] = (even - odd) * HAAR
    v = sq[0]
    tb[1, 0] = (v * sigmoid(v)).astype(BF16)
    tb[1, 1] = sq[1].astype(BF16)
    pl.semaphore_wait(barrier, met)

    ahead_t = send(tb.at[1], tb.at[0], t_snd.at[0], t_rcv.at[0], ((tm + 1) % 32, row))
    behind_t = send(tb.at[1], tb.at[2], t_snd.at[1], t_rcv.at[1], ((tm + 31) % 32, row))
    has_next, has_last = jnp.logical_not(last_t), jnp.logical_not(first_t)
    pl.when(has_next)(ahead_t.start)
    pl.when(has_last)(behind_t.start)

    def time_taps(ks):
        for q in range(5):
            at = pl.ds(q * 128, 128)
            ahead, back = None, None
            for k in ks:
                one = dot(tb[k, 0, :, at], wt[k, q], 1, 0)
                two = dot(tb[2 - k, 1, :, at], wt[k, q], 1, 1)
                ahead, back = (one, two) if ahead is None else (ahead + one, back + two)
            yield at, ahead, back

    def time_terms(ks):
        for k in ks:
            for q in range(5):
                at = pl.ds(q * 128, 128)
                gt[pl.ds((k * 5 + q) * 16, 16)] = dot(tb[1, 0, :, at], tb[2 - k, 1, :, at], 0, 0).reshape(16, 8, 128)

    loads[2].wait()
    for at, ahead, back in time_taps((1,)):
        cs[0, :, at] = ahead
        cs[1, :, at] = back
    time_terms((1,))
    loads[3].wait()
    loads[4].wait()
    pl.when(has_last)(ahead_t.wait_recv)
    pl.when(has_next)(behind_t.wait_recv)
    for at, ahead, back in time_taps((0, 2)):
        cs[0, :, at] = cs[0, :, at] + ahead
        cs[1, :, at] = (cs[1, :, at] + back) * slope(sq[0, :, at])
    for n, (src, res) in enumerate(((y2, xs), (c1, gf))):
        low, high = cs[n, :, 0:320], cs[n, :, 320:640]
        for f in range(2):
            part = ((low + high if f == 0 else low - high) * HAAR).astype(BF16).astype(F32)
            new = (src[f].astype(F32) - part if n == 0 else src[f].astype(F32) + part).astype(BF16)
            res[f] = new
            held = new
            if n == 0:
                w = new.astype(F32)
                held = (w * sigmoid(w)).astype(BF16)
            hb[own, n, pl.ds(f * 64, 64)] = held
    far_row = send(hb.at[own], hb.at[3 - far], r_snd.at[0], r_rcv.at[0], (tm, (row + 2 * c + 15) % 16))
    pl.when(has_far)(far_row.start)
    near_row = send(hb.at[own], hb.at[own], n_snd.at[0], n_rcv.at[0], partner)
    near_row.start()

    time_terms((0, 2))

    def pack_time(n, carry):
        chunk = (n // 4 + 8 - SHIFT) % 8 * 4 + n % 4
        tiles = gt[pl.ds((15 * chunk) // 2, 8)].astype(BF16)

        def put(ref, m):
            ref[m, n % 4, n // 4] = tiles[0:3]
            ref[m + 1, n % 4, n // 4] = tiles[3:6]
            ref[m + 2, n % 4, n // 4, 0:2] = tiles[6:8]
            ref[m + 2, n % 4, n // 4, 2:3] = jnp.zeros((1, 8, 128), BF16)

        pl.when(c == 0)(lambda: put(rt, 0))
        pl.when(c == 1)(lambda: put(s0, 1))
        return carry

    lax.fori_loop(0, 32, pack_time, 0)
    time_half = [send(rt.at[xp - 1], rt.at[xp - 1], q_snd.at[xp - 1], q_rcv.at[xp - 1], partner) for xp in (1, 2, 3)]

    @pl.when(c == 0)
    def _():
        for copy in time_half:
            copy.start()

    def spread(slot):
        for n, ref in enumerate((pa, pg)):
            wide[n] = hb[slot, n].astype(F32)
            for q in range(2):
                ref[slot, q, :, 8:72] = wide[n, :, pl.ds(q * 160, 160)].reshape(2, 64, 160)

    def right_side(slot):
        for q in range(2):
            for n in range(4):
                rq[q, slot - 1, :, pl.ds(32 * n, 32)] = jnp.where(
                    c == 0, wide[1, :, pl.ds(q * 160 + 32 * n, 32)], wide[1, :, pl.ds(q * 160 + 128, 32)]
                ).astype(BF16)

    spread(own)
    near_row.wait_recv()
    spread(other)
    for slot in (1, 2):
        wide[1] = hb[slot, 1].astype(F32)
        right_side(slot)

    def left(slot, b, q):
        return pa[slot, q, :, pl.ds(7 + b, 64)].reshape(128, 160).astype(BF16)

    def space_terms(rows):
        for q in range(2):
            for a in rows:
                for b in range(3):
                    tap = a * 3 + b
                    both = jnp.concatenate([left(a, b, q), left(a + 1, b, q)], axis=0)
                    g[pl.ds((tap * 2 + q) * 20, 20)] = dot(both, rq[q].reshape(256, 128), 0, 0).reshape(20, 8, 128)

    lane = lax.broadcasted_iota(jnp.int32, (3, 8, 128), 2)

    def pack_space(lo, hi):
        def pack(n, carry):
            zz, yp = n // 4, n % 4
            chunk = (zz + 8 - SHIFT) % 8 * 4 + yp
            tiles = g[pl.ds((45 * chunk) // 4, 12)]

            @pl.when(c == 0)
            def _():
                for m in range(4):
                    s0[m, yp, zz] = tiles[3 * m : 3 * m + 3].astype(BF16)

            @pl.when(c == 1)
            def _():
                one, two = jnp.where(lane < 32, tiles[0:3], tiles[3:6]), jnp.where(lane < 96, tiles[6:9], tiles[9:12])
                s0[0, yp, zz] = jnp.where(lane < 64, one, two).astype(BF16)

            return carry

        lax.fori_loop(lo * 4, hi * 4, pack, 0)

    def along_x(k, j, part):
        xp, yp = (x + k) % 4, (yl + j) % 4
        at = pl.ds(0, EARLY) if part == 0 else pl.ds(EARLY, 8 - EARLY)
        return send(s0.at[xp, yp, at], r1.at[k - 1, yp, at], x_snd.at[k - 1, j, part], x_rcv.at[k - 1, j, part], ident(z, yl, xp, yh, c))

    space_terms((1,))

    @pl.when(c == 1)
    def _():
        for xp in (1, 2, 3):
            time_half[xp - 1].wait_recv()
            for yp in range(4):
                s0[xp, yp] = (s0[xp, yp].astype(F32) + rt[xp - 1, yp].astype(F32)).astype(BF16)

    pack_space(0, EARLY)
    timed = [jnp.logical_and(c == 1, (x + k) % 4 != 0) for k in range(4)]
    for k in (1, 2, 3):
        for j in (1, 2, 3, 0):
            along_x(k, j, 0).start()
            pl.when(timed[k])(along_x(k, j, 1).start)

    pl.when(has_far)(far_row.wait_recv)
    pass_on = send(hb.at[far, 0], hb.at[far, 0], f_snd.at[0], f_rcv.at[0], partner)
    pass_on.start()
    spread(far)
    for q in range(2):
        ahead, back = None, None
        for a in range(3):
            for b in range(3):
                moved = left(c + a, b, q)
                one = dot(moved, ws_at(ws, loads, a, b, q), 1, 0)
                moved = pg[c + 2 - a, q, :, pl.ds(9 - b, 64)].reshape(128, 160).astype(BF16)
                two = dot(moved, ws[a, b, q], 1, 1)
                ahead, back = (one, two) if ahead is None else (ahead + one, back + two)
        sa[0, :, pl.ds(q * 160, 160)] = ahead
        sa[1, :, pl.ds(q * 160, 160)] = back
    pass_on.wait_recv()
    wide[0] = hb[3 - far, 0].astype(F32)
    for q in range(2):
        pa[3 - far, q, :, 8:72] = wide[0, :, pl.ds(q * 160, 160)].reshape(2, 64, 160)
    space_terms((0, 2))
    pack_space(EARLY, 8)
    for k in (1, 2, 3):
        for j in (1, 2, 3, 0):
            pl.when(jnp.logical_not(timed[k]))(along_x(k, j, 1).start)
    for f in range(2):
        at = pl.ds(f * 64, 64)
        xf[f] = (y1[f].astype(F32) - sa[0, at]).astype(BF16)
        gs[f] = (c2[f].astype(F32) + sa[1, at] * slope(xs[f].astype(F32))).astype(BF16)

    third = {}
    for j in (1, 2, 3, 0):
        yp = (yl + j) % 4
        for k in (1, 2, 3):
            for part in range(2):
                along_x(k, j, part).wait_recv()
        total = s0[x, yp].astype(F32)
        for k in (1, 2, 3):
            total += r1[k - 1, yp].astype(F32)
        s1[yp] = total.astype(BF16)
        for h in (1, 0):
            if j or h:
                hp = (yh + h) % 2
                copy = send(s1.at[yp, pl.ds(hp * 4, 4)], r2.at[2 * j + h], y_snd.at[2 * j + h], y_rcv.at[2 * j + h], ident(z, yp, x, hp, c))
                copy.start()
                third[j, h] = copy
    total = s1[yl, pl.ds(yh * 4, 4)].astype(F32)
    for j, h in third:
        third[j, h].wait_recv()
    for j, h in third:
        total += r2[2 * j + h].astype(F32)
    s2[...] = total.astype(BF16)

    mine = (z + SHIFT) % 8 // 4 == yh

    def along_z(d, finish):
        zp = (z + d) % 8
        zz = (zp + SHIFT) % 8
        copy = send(s2.at[zz % 4], r3.at[d - 1], z_snd.at[d - 1], z_rcv.at[d - 1], ident(zp, yl, x, yh, c))
        pl.when(zz // 4 == yh)(copy.wait_send if finish else copy.start)

    def over_row(finish):
        for dx in range(4):
            for h in range(2):
                for dc in range(2):
                    if dx or h or dc:
                        n = dx * 2 + dc
                        copy = send(fin.at[c * 4 + x], fin.at[c * 4 + x], g_snd.at[n, h], g_rcv.at[n], ident(z, yl, (x + dx) % 4, (yh + h) % 2, (c + dc) % 2))
                        copy.wait_send() if finish else copy.start()

    for d in range(1, 8):
        along_z(d, False)

    @pl.when(mine)
    def _():
        for d in range(1, 8):
            send(s2.at[0], r3.at[d - 1], z_snd.at[d - 1], z_rcv.at[d - 1], ident((z + d) % 8, yl, x, yh, c)).wait_recv()
        last = s2[(z + SHIFT) % 4].astype(F32)
        for d in range(1, 8):
            last += r3[d - 1].astype(F32)
        fin[c * 4 + x] = last
        over_row(False)

    pl.when(has_next)(ahead_t.wait_send)
    pl.when(has_last)(behind_t.wait_send)
    pl.when(has_far)(far_row.wait_send)
    near_row.wait_send()
    pass_on.wait_send()

    @pl.when(c == 0)
    def _():
        for copy in time_half:
            copy.wait_send()

    for k in (1, 2, 3):
        for j in range(4):
            for part in range(2):
                along_x(k, j, part).wait_send()
    for copy in third.values():
        copy.wait_send()
    for d in range(1, 8):
        along_z(d, True)

    for dx in range(4):
        for dc in range(2):
            n = dx * 2 + dc
            src = (c + dc) % 2 * 4 + (x - dx) % 4
            copy = send(fin.at[src], fin.at[src], g_snd.at[n, 1], g_rcv.at[n], ident(z, yl, (x + dx) % 4, 1 - yh, (c + dc) % 2))
            if n:
                copy.wait_recv()
            else:
                pl.when(jnp.logical_not(mine))(copy.wait_recv)
    out[...] = fin[...]
    pl.when(mine)(lambda: over_row(True))


def ws_at(ws, loads, a, b, q):
    if (a, b, q) == (0, 0, 0):
        loads[5].wait()
    return ws[a, b, q]


def block(y1, y2, c1, c2, ws, wt):
    dma = pltpu.SemaphoreType.DMA
    here, there = pl.BlockSpec(memory_space=pltpu.VMEM), pl.BlockSpec(memory_space=pl.ANY)
    one = jax.ShapeDtypeStruct((2, 64, 320), BF16)
    vm = pltpu.VMEM
    return pl.pallas_call(
        block_kernel,
        out_shape=[one] * 4 + [jax.ShapeDtypeStruct((8, 3, 8, 128), F32)],
        in_specs=[there] * 6,
        out_specs=[here] * 5,
        scratch_shapes=[vm((2, 64, 320), BF16)] * 4
        + [
            vm((3, 3, 2, 160, 160), BF16),
            vm((3, 5, 128, 128), BF16),
            vm((3, 2, 64, 640), BF16),
            vm((4, 2, 128, 320), BF16),
            vm((2, 64, 640), F32),
            vm((2, 64, 640), F32),
            vm((2, 128, 320), F32),
            vm((4, 2, 2, 80, 160), F32),
            vm((4, 2, 2, 80, 160), F32),
            vm((2, 128, 320), F32),
            vm((2, 2, 128, 128), BF16),
            vm((360, 8, 128), F32),
            vm((240, 8, 128), F32),
            vm((3, 4, 8, 3, 8, 128), BF16),
            vm((4, 4, 8, 3, 8, 128), BF16),
            vm((3, 4, 8, 3, 8, 128), BF16),
            vm((4, 8, 3, 8, 128), BF16),
            vm((8, 4, 3, 8, 128), BF16),
            vm((4, 3, 8, 128), BF16),
            vm((7, 3, 8, 128), BF16),
            vm((8, 3, 8, 128), F32),
        ]
        + [dma((6,))]
        + [dma((2,))] * 2
        + [dma((1,))] * 6
        + [dma((3,))] * 2
        + [dma((3, 4, 2))] * 2
        + [dma((8,))] * 2
        + [dma((7,))] * 2
        + [dma((8, 2)), dma((8,))],
        compiler_params=pltpu.CompilerParams(collective_id=5, has_side_effects=True, vmem_limit_bytes=60 * 1024 * 1024),
        name="block",
    )(y1, y2, c1, c2, ws, wt)


def tail_kernel(factor, xf, xs, gf, gs, chunk, xf_o, xs_o, gf_o, gs_o, space, time, rest, line):
    tm, row = lax.axis_index("tm"), lax.axis_index("row")
    for src, dst in ((xf, xf_o), (xs, xs_o), (gf, gf_o), (gs, gs_o)):
        dst[...] = src[...]
    four = chunk[4].reshape(24, 128)
    for n in range(4):
        rest[pl.ds(24 * n, 24), 0:32] = four[:, 32 * n : 32 * n + 32]
    flat = 900 * row
    start = 90 * tm % 8 + flat // 160
    main = pltpu.roll(chunk[0:4].reshape(96, 128), (96 - start) % 96, 0)
    side = pltpu.roll(rest[...], (96 - start) % 96, 0)
    for n in range(7):
        line[0:1, pl.ds(160 * n, 128)] = main[n : n + 1]
        line[0:1, pl.ds(160 * n + 128, 32)] = side[n : n + 1, 0:32]
    space[...] = pltpu.roll(line[...], (1280 - flat % 160) % 1280, 1)[0:1, 0:900] * factor
    flat = 480 * row
    start = 60 * tm % 8 + flat // 128
    main = pltpu.roll(chunk[5:8].reshape(72, 128), (72 - start) % 72, 0)
    for n in range(5):
        line[0:1, pl.ds(128 * n, 128)] = main[n : n + 1]
    time[...] = pltpu.roll(line[...], (1280 - flat % 128) % 1280, 1)[0:1, 0:480] * factor


def tail(factor, outs, chunk):
    here = pl.BlockSpec(memory_space=pltpu.VMEM)
    one = jax.ShapeDtypeStruct((2, 64, 320), BF16)
    return pl.pallas_call(
        lambda *refs: tail_kernel(factor, *refs),
        out_shape=[one] * 4 + [jax.ShapeDtypeStruct((1, 900), F32), jax.ShapeDtypeStruct((1, 480), F32)],
        in_specs=[here] * 5,
        out_specs=[here] * 6,
        scratch_shapes=[pltpu.VMEM((96, 128), F32), pltpu.VMEM((8, 1280), F32)],
        name="tail",
    )(*outs, chunk)


def per_device(output_first_half, y_second, cot_first, cot_second, weight_space, temporal_weight):
    cells_all = (
        output_first_half.shape[0]
        * output_first_half.shape[1]
        * output_first_half.shape[2]
        * lax.axis_size("tm")
        * lax.axis_size("row")
    )
    factor = 1.0 / math.sqrt(cells_all)
    flat = [v.reshape(2, 64, 320) for v in (output_first_half, y_second, cot_first, cot_second)]
    *outs, chunk = block(*flat, weight_space, temporal_weight)
    *outs, space, time = tail(factor, outs, chunk)
    return tuple(v.reshape(output_first_half.shape) for v in outs) + (space.reshape(-1), time.reshape(-1))


def solution(mesh):
    in_specs = (
        P("tm", "row", None, None),
        P("tm", "row", None, None),
        P("tm", "row", None, None),
        P("tm", "row", None, None),
        P(),
        P(),
    )
    out_specs = (
        P("tm", "row", None, None),
        P("tm", "row", None, None),
        P("tm", "row", None, None),
        P("tm", "row", None, None),
        P(("tm", "row")),
        P(("tm", "row")),
    )
    return jax.shard_map(
        per_device, mesh=mesh, in_specs=in_specs, out_specs=out_specs, check_vma=False
    )
```

```python
import math

import jax
import jax.numpy as jnp
from jax import lax
from jax.experimental import pallas as pl
from jax.experimental.pallas import tpu as pltpu
from jax.sharding import PartitionSpec as P

MESH = pl.DeviceIdType.MESH
F32, BF16 = jnp.float32, jnp.bfloat16
HAAR = 0.7071067811865476
SHIFT, EARLY = 5, 2


def place():
    tm, row = lax.axis_index("tm"), lax.axis_index("row")
    return tm // 4, tm % 4, row // 4, (row // 2) % 2, row % 2


def ident(z, yl, x, yh, c):
    return (z * 4 + yl, x * 4 + yh * 2 + c)


def sigmoid(v):
    return 1.0 / (1.0 + jnp.exp(-v))


def slope(v):
    s = sigmoid(v)
    return s * (1.0 + v * (1.0 - s))


def dot(a, b, ca, cb):
    return lax.dot_general(a, b, (((ca,), (cb,)), ((), ())), preferred_element_type=F32)


def send(src, dst, snd, rcv, peer):
    return pltpu.make_async_remote_copy(
        src_ref=src, dst_ref=dst, send_sem=snd, recv_sem=rcv, device_id=peer, device_id_type=MESH
    )


def greet(z, yl, x, yh, c):
    tm, row = z * 4 + yl, x * 4 + yh * 2 + c
    peers = [((tm + 1) % 32, row), ((tm + 31) % 32, row), (tm, (row + 2 * c + 15) % 16)]
    for dx in range(4):
        for h in range(2):
            for dc in range(2):
                if dx or h or dc:
                    peers.append(ident(z, yl, (x + dx) % 4, (yh + h) % 2, (c + dc) % 2))
    for j in range(1, 4):
        for h in range(2):
            peers.append(ident(z, (yl + j) % 4, x, (yh + h) % 2, c))
    for d in range(1, 8):
        peers.append(ident((z + d) % 8, yl, x, yh, c))
    barrier = pltpu.get_barrier_semaphore()
    for peer in peers:
        pl.semaphore_signal(barrier, inc=1, device_id=peer, device_id_type=MESH)
    return barrier, len(peers)


def block_kernel(
    y1h, y2h, c1h, c2h, wsh, wth, xf, xs, gf, gs, out,
    y1, y2, c1, c2, ws, wt, tb, hb, sq, cs, wide, pa, pg, rq, g, gt, rt, s0, r1, s1, r2, s2, r3, fin,
    in_sem, t_snd, t_rcv, n_snd, n_rcv, r_snd, r_rcv, f_snd, f_rcv, q_snd, q_rcv, x_snd, x_rcv, y_snd, y_rcv, z_snd, z_rcv, g_snd, g_rcv,
):
    z, yl, x, yh, c = place()
    tm, row = z * 4 + yl, x * 4 + yh * 2 + c
    loads = [
        pltpu.make_async_copy(src, dst, in_sem.at[n])
        for n, (src, dst) in enumerate(((y1h, y1), (c2h, c2), (wth, wt), (y2h, y2), (c1h, c1), (wsh, ws)))
    ]
    for load in loads:
        load.start()
    barrier, met = greet(z, yl, x, yh, c)
    partner = ident(z, yl, x, yh, 1 - c)
    first_t, last_t = tm == 0, tm == 31
    own, other, far = 1 + c, 2 - c, 3 * c
    has_far = jnp.logical_not(jnp.logical_or(row == 0, row == 15))
    pad = jnp.zeros((4, 2, 2, 8, 160), F32)
    for ref in (pa, pg):
        ref[:, :, :, 0:8] = pad
        ref[:, :, :, 72:80] = pad

    @pl.when(first_t)
    def _():
        tb[0] = jnp.zeros((2, 64, 640), BF16)

    @pl.when(last_t)
    def _():
        tb[2] = jnp.zeros((2, 64, 640), BF16)

    @pl.when(jnp.logical_not(has_far))
    def _():
        hb[far] = jnp.zeros((2, 5, 64, 128), BF16)

    for n, ref in enumerate((y1, c2)):
        loads[n].wait()
        even, odd = ref[0].astype(F32), ref[1].astype(F32)
        sq[n, :, 0:320] = (even + odd) * HAAR
        sq[n, :, 320:640] = (even - odd) * HAAR
    v = sq[0]
    tb[1, 0] = (v * sigmoid(v)).astype(BF16)
    tb[1, 1] = sq[1].astype(BF16)
    pl.semaphore_wait(barrier, met)

    ahead_t = [send(tb.at[1, n], tb.at[0, n], t_snd.at[n, 0], t_rcv.at[n, 0], ((tm + 1) % 32, row)) for n in range(2)]
    behind_t = [send(tb.at[1, n], tb.at[2, n], t_snd.at[n, 1], t_rcv.at[n, 1], ((tm + 31) % 32, row)) for n in range(2)]
    has_next, has_last = jnp.logical_not(last_t), jnp.logical_not(first_t)
    for n in range(2):
        pl.when(has_next)(ahead_t[n].start)
        pl.when(has_last)(behind_t[n].start)

    def time_taps(n, ks, q):
        at = pl.ds(q * 128, 128)
        both = None
        for k in ks:
            one = dot(tb[k, 0, :, at], wt[k, q], 1, 0) if n == 0 else dot(tb[2 - k, 1, :, at], wt[k, q], 1, 1)
            both = one if both is None else both + one
        return both

    def time_terms(ks):
        for k in ks:
            for q in range(5):
                at = pl.ds(q * 128, 128)
                gt[pl.ds((k * 5 + q) * 16, 16)] = dot(tb[1, 0, :, at], tb[2 - k, 1, :, at], 0, 0).reshape(16, 8, 128)

    loads[2].wait()
    for n in range(2):
        for q in range(5):
            cs[n, :, pl.ds(q * 128, 128)] = time_taps(n, (1,), q)
    time_terms((1,))
    loads[3].wait()
    loads[4].wait()
    far_row, near_row = [], []
    for n, (src, res) in enumerate(((y2, xs), (c1, gf))):
        pl.when(has_last)(ahead_t[n].wait_recv)
        pl.when(has_next)(behind_t[n].wait_recv)
        for q in range(5):
            at = pl.ds(q * 128, 128)
            whole = cs[n, :, at] + time_taps(n, (0, 2), q)
            cs[n, :, at] = whole if n == 0 else whole * slope(sq[0, :, at])
        low, high = cs[n, :, 0:320], cs[n, :, 320:640]
        for f in range(2):
            part = ((low + high if f == 0 else low - high) * HAAR).astype(BF16).astype(F32)
            new = (src[f].astype(F32) - part if n == 0 else src[f].astype(F32) + part).astype(BF16)
            res[f] = new
            held = new
            if n == 0:
                w = new.astype(F32)
                held = (w * sigmoid(w)).astype(BF16)
            hb[own, n, 2 * f] = held[:, 0:128]
            hb[own, n, 2 * f + 1] = held[:, 128:256]
            hb[own, n, 4, :, pl.ds(64 * f, 64)] = held[:, 256:320]
        far_row.append(send(hb.at[own, n], hb.at[3 - far, n], r_snd.at[n], r_rcv.at[n], (tm, (row + 2 * c + 15) % 16)))
        pl.when(has_far)(far_row[n].start)
        near_row.append(send(hb.at[own, n], hb.at[own, n], n_snd.at[n], n_rcv.at[n], partner))
        near_row[n].start()

    time_terms((0, 2))

    def pack_time(n, carry):
        chunk = (n // 4 + 8 - SHIFT) % 8 * 4 + n % 4
        tiles = gt[pl.ds((15 * chunk) // 2, 8)].astype(BF16)

        def put(ref, m):
            ref[m, n % 4, n // 4] = tiles[0:3]
            ref[m + 1, n % 4, n // 4] = tiles[3:6]
            ref[m + 2, n % 4, n // 4, 0:2] = tiles[6:8]
            ref[m + 2, n % 4, n // 4, 2:3] = jnp.zeros((1, 8, 128), BF16)

        pl.when(c == 0)(lambda: put(rt, 0))
        pl.when(c == 1)(lambda: put(s0, 1))
        return carry

    lax.fori_loop(0, 32, pack_time, 0)
    time_half = [send(rt.at[xp - 1], rt.at[xp - 1], q_snd.at[xp - 1], q_rcv.at[xp - 1], partner) for xp in (1, 2, 3)]

    @pl.when(c == 0)
    def _():
        for copy in time_half:
            copy.start()

    def widen(slot, n):
        for f in range(2):
            at = pl.ds(f * 64, 64)
            wide[n, at, 0:128] = hb[slot, n, 2 * f].astype(F32)
            wide[n, at, 128:256] = hb[slot, n, 2 * f + 1].astype(F32)
            wide[n, at, 256:320] = hb[slot, n, 4, :, pl.ds(64 * f, 64)].astype(F32)

    def spread(slot, n):
        widen(slot, n)
        for q in range(2):
            (pa, pg)[n][slot, q, :, 8:72] = wide[n, :, pl.ds(q * 160, 160)].reshape(2, 64, 160)

    def right_side(slot):
        for q in range(2):
            for n in range(4):
                rq[q, slot - 1, :, pl.ds(32 * n, 32)] = jnp.where(
                    c == 0, wide[1, :, pl.ds(q * 160 + 32 * n, 32)], wide[1, :, pl.ds(q * 160 + 128, 32)]
                ).astype(BF16)

    for slot in (own, other):
        for n in range(2):
            if slot is other:
                near_row[n].wait_recv()
            spread(slot, n)
        right_side(slot)

    def left(slot, b, q):
        return pa[slot, q, :, pl.ds(7 + b, 64)].reshape(128, 160).astype(BF16)

    def space_terms(rows):
        for q in range(2):
            for a in rows:
                for b in range(3):
                    tap = a * 3 + b
                    both = jnp.concatenate([left(a, b, q), left(a + 1, b, q)], axis=0)
                    g[pl.ds((tap * 2 + q) * 20, 20)] = dot(both, rq[q].reshape(256, 128), 0, 0).reshape(20, 8, 128)

    lane = lax.broadcasted_iota(jnp.int32, (3, 8, 128), 2)

    def pack_space(lo, count):
        def pack(n, carry):
            zz, yp = lo + n // 4, n % 4
            chunk = (zz + 8 - SHIFT) % 8 * 4 + yp
            tiles = g[pl.ds((45 * chunk) // 4, 12)]

            @pl.when(c == 0)
            def _():
                for m in range(4):
                    s0[m, yp, zz] = tiles[3 * m : 3 * m + 3].astype(BF16)

            @pl.when(c == 1)
            def _():
                one, two = jnp.where(lane < 32, tiles[0:3], tiles[3:6]), jnp.where(lane < 96, tiles[6:9], tiles[9:12])
                s0[0, yp, zz] = jnp.where(lane < 64, one, two).astype(BF16)

            return carry

        lax.fori_loop(0, count * 4, pack, 0)

    def group(xp, yp):
        return (xp + 4 - yp) % 4

    def along_x(k, j, part):
        xp, yp = (x + k) % 4, (yl + j) % 4
        at = pl.ds(0, EARLY) if isinstance(part, int) and part == 0 else pl.ds(EARLY + 3 * (part - 1), 3)
        return send(s0.at[group(xp, yp), yp, at], r1.at[k - 1, yp, at], x_snd.at[k - 1, j, part], x_rcv.at[k - 1, j, part], ident(z, yl, xp, yh, c))

    space_terms((1,))

    @pl.when(c == 1)
    def _():
        for xp in (1, 2, 3):
            time_half[xp - 1].wait_recv()
            for yp in range(4):
                s0[xp, yp] = (s0[xp, yp].astype(F32) + rt[xp - 1, yp].astype(F32)).astype(BF16)

    pack_space(0, EARLY)
    order = [(k, j) for j in (1, 2, 3, 0) for k in (2, 1, 3)]
    timed = {(k, j): jnp.logical_and(c == 1, group((x + k) % 4, (yl + j) % 4) != 0) for k, j in order}
    for k, j in order:
        along_x(k, j, 0).start()

        @pl.when(timed[k, j])
        def _():
            along_x(k, j, 1).start()
            along_x(k, j, 2).start()

    def late_part(part):
        pack_space(EARLY + 3 * (part - 1), 3)
        for k, j in order:
            pl.when(jnp.logical_not(timed[k, j]))(along_x(k, j, part).start)


    pl.when(has_far)(far_row[0].wait_recv)
    pass_on = send(hb.at[far, 0], hb.at[far, 0], f_snd.at[0], f_rcv.at[0], partner)
    pass_on.start()
    spread(far, 0)
    space_terms((2 * c,))
    late_part(2 - c)
    pass_on.wait_recv()
    spread(3 - far, 0)
    space_terms((2 - 2 * c,))
    late_part(1 + c)

    def along_y(j, h):
        yp, hp = (yl + j) % 4, (yh + h) % 2
        return send(s1.at[yp, pl.ds(hp * 4, 4)], r2.at[2 * j + h], y_snd.at[2 * j + h], y_rcv.at[2 * j + h], ident(z, yp, x, hp, c))

    def sum_x(j):
        yp = (yl + j) % 4
        for k in (1, 2, 3):
            for part in range(3):
                along_x(k, j, part).wait_recv()
        total = s0[group(x, yp), yp].astype(F32)
        for k in (1, 2, 3):
            total += r1[k - 1, yp].astype(F32)
        s1[yp] = total.astype(BF16)
        for h in (1, 0):
            if j or h:
                along_y(j, h).start()

    for early in (True, False):
        for j in (1, 2, 3, 0):
            is_time = jnp.logical_and(c == 1, group(x, (yl + j) % 4) != 0)
            pl.when(is_time if early else jnp.logical_not(is_time))(lambda j=j: sum_x(j))

    pl.when(has_far)(far_row[1].wait_recv)
    spread(far, 1)
    loads[5].wait()
    for q in range(2):
        ahead, back = None, None
        for a in range(3):
            for b in range(3):
                one = dot(left(c + a, b, q), ws[a, b, q], 1, 0)
                moved = pg[c + 2 - a, q, :, pl.ds(9 - b, 64)].reshape(128, 160).astype(BF16)
                two = dot(moved, ws[a, b, q], 1, 1)
                ahead, back = (one, two) if ahead is None else (ahead + one, back + two)
        wide[0, :, pl.ds(q * 160, 160)] = ahead
        wide[1, :, pl.ds(q * 160, 160)] = back
    for f in range(2):
        at = pl.ds(f * 64, 64)
        xf[f] = (y1[f].astype(F32) - wide[0, at]).astype(BF16)
        gs[f] = (c2[f].astype(F32) + wide[1, at] * slope(xs[f].astype(F32))).astype(BF16)

    total = s1[yl, pl.ds(yh * 4, 4)].astype(F32)
    others = [(j, h) for j in (1, 2, 3, 0) for h in (1, 0) if j or h]
    for j, h in others:
        along_y(j, h).wait_recv()
    for j, h in others:
        total += r2[2 * j + h].astype(F32)
    s2[...] = total.astype(BF16)

    mine = (z + SHIFT) % 8 // 4 == yh

    def along_z(d, finish):
        zp = (z + d) % 8
        zz = (zp + SHIFT) % 8
        copy = send(s2.at[zz % 4], r3.at[d - 1], z_snd.at[d - 1], z_rcv.at[d - 1], ident(zp, yl, x, yh, c))
        pl.when(zz // 4 == yh)(copy.wait_send if finish else copy.start)

    def takes(slot, to):
        space, time = 90 * tm % 8 + 900 * to // 160, 60 * tm % 8 + 480 * to // 128
        low = 24 * (slot % 5)
        main = jnp.logical_and(space <= low + 23, space + 6 >= low)
        late = jnp.logical_and(time <= low + 23, time + 4 >= low)
        return jnp.logical_or(slot == 4, jnp.logical_or(jnp.logical_and(slot < 4, main), jnp.logical_and(slot > 4, late)))

    offsets = [(dx, h, dc) for dx in (2, 1, 3, 0) for h in (1, 0) for dc in (1, 0) if dx or h or dc]

    def over_row(finish):
        slot = c * 4 + group(x, yl)
        for dx, h, dc in offsets:
            n, xp, hp, cp = dx * 2 + dc, (x + dx) % 4, (yh + h) % 2, (c + dc) % 2
            copy = send(fin.at[slot], fin.at[slot], g_snd.at[n, h], g_rcv.at[n], ident(z, yl, xp, hp, cp))
            pl.when(takes(slot, xp * 4 + hp * 2 + cp))(copy.wait_send if finish else copy.start)

    for d in range(1, 8):
        along_z(d, False)

    @pl.when(mine)
    def _():
        for d in range(1, 8):
            send(s2.at[0], r3.at[d - 1], z_snd.at[d - 1], z_rcv.at[d - 1], ident((z + d) % 8, yl, x, yh, c)).wait_recv()
        last = s2[(z + SHIFT) % 4].astype(F32)
        for d in range(1, 8):
            last += r3[d - 1].astype(F32)
        fin[c * 4 + group(x, yl)] = last
        over_row(False)

    for n in range(2):
        pl.when(has_next)(ahead_t[n].wait_send)
        pl.when(has_last)(behind_t[n].wait_send)
        pl.when(has_far)(far_row[n].wait_send)
        near_row[n].wait_send()
    pass_on.wait_send()

    @pl.when(c == 0)
    def _():
        for copy in time_half:
            copy.wait_send()

    for k in (1, 2, 3):
        for j in range(4):
            for part in range(3):
                along_x(k, j, part).wait_send()
    for j, h in others:
        along_y(j, h).wait_send()
    for d in range(1, 8):
        along_z(d, True)

    for dx in range(4):
        for dc in range(2):
            n = dx * 2 + dc
            src = (c + dc) % 2 * 4 + group((x + 4 - dx) % 4, yl)
            copy = send(fin.at[src], fin.at[src], g_snd.at[n, 1], g_rcv.at[n], ident(z, yl, (x + dx) % 4, 1 - yh, (c + dc) % 2))
            wanted = takes(src, row)
            pl.when(wanted if n else jnp.logical_and(wanted, jnp.logical_not(mine)))(copy.wait_recv)
    out[...] = fin[...]
    pl.when(mine)(lambda: over_row(True))


def block(y1, y2, c1, c2, ws, wt):
    dma = pltpu.SemaphoreType.DMA
    here, there = pl.BlockSpec(memory_space=pltpu.VMEM), pl.BlockSpec(memory_space=pl.ANY)
    one = jax.ShapeDtypeStruct((2, 64, 320), BF16)
    vm = pltpu.VMEM
    return pl.pallas_call(
        block_kernel,
        out_shape=[one] * 4 + [jax.ShapeDtypeStruct((8, 3, 8, 128), F32)],
        in_specs=[there] * 6,
        out_specs=[here] * 5,
        scratch_shapes=[vm((2, 64, 320), BF16)] * 4
        + [
            vm((3, 3, 2, 160, 160), BF16),
            vm((3, 5, 128, 128), BF16),
            vm((3, 2, 64, 640), BF16),
            vm((4, 2, 5, 64, 128), BF16),
            vm((2, 64, 640), F32),
            vm((2, 64, 640), F32),
            vm((2, 128, 320), F32),
            vm((4, 2, 2, 80, 160), F32),
            vm((4, 2, 2, 80, 160), F32),
            vm((2, 2, 128, 128), BF16),
            vm((360, 8, 128), F32),
            vm((240, 8, 128), F32),
            vm((3, 4, 8, 3, 8, 128), BF16),
            vm((4, 4, 8, 3, 8, 128), BF16),
            vm((3, 4, 8, 3, 8, 128), BF16),
            vm((4, 8, 3, 8, 128), BF16),
            vm((8, 4, 3, 8, 128), BF16),
            vm((4, 3, 8, 128), BF16),
            vm((7, 3, 8, 128), BF16),
            vm((8, 3, 8, 128), F32),
        ]
        + [dma((6,))]
        + [dma((2, 2))] * 2
        + [dma((2,))] * 4
        + [dma((1,))] * 2
        + [dma((3,))] * 2
        + [dma((3, 4, 3))] * 2
        + [dma((8,))] * 2
        + [dma((7,))] * 2
        + [dma((8, 2)), dma((8,))],
        compiler_params=pltpu.CompilerParams(collective_id=5, has_side_effects=True, vmem_limit_bytes=60 * 1024 * 1024),
        name="block",
    )(y1, y2, c1, c2, ws, wt)


def tail_kernel(factor, xf, xs, gf, gs, chunk, xf_o, xs_o, gf_o, gs_o, space, time, rest, line):
    tm, row = lax.axis_index("tm"), lax.axis_index("row")
    for src, dst in ((xf, xf_o), (xs, xs_o), (gf, gf_o), (gs, gs_o)):
        dst[...] = src[...]
    four = chunk[4].reshape(24, 128)
    for n in range(4):
        rest[pl.ds(24 * n, 24), 0:32] = four[:, 32 * n : 32 * n + 32]
    flat = 900 * row
    start = 90 * tm % 8 + flat // 160
    main = pltpu.roll(chunk[0:4].reshape(96, 128), (96 - start) % 96, 0)
    side = pltpu.roll(rest[...], (96 - start) % 96, 0)
    for n in range(7):
        line[0:1, pl.ds(160 * n, 128)] = main[n : n + 1]
        line[0:1, pl.ds(160 * n + 128, 32)] = side[n : n + 1, 0:32]
    space[...] = pltpu.roll(line[...], (1280 - flat % 160) % 1280, 1)[0:1, 0:900] * factor
    flat = 480 * row
    start = 60 * tm % 8 + flat // 128
    main = pltpu.roll(chunk[5:8].reshape(72, 128), (72 - start) % 72, 0)
    for n in range(5):
        line[0:1, pl.ds(128 * n, 128)] = main[n : n + 1]
    time[...] = pltpu.roll(line[...], (1280 - flat % 128) % 1280, 1)[0:1, 0:480] * factor


def tail(factor, outs, chunk):
    here = pl.BlockSpec(memory_space=pltpu.VMEM)
    one = jax.ShapeDtypeStruct((2, 64, 320), BF16)
    return pl.pallas_call(
        lambda *refs: tail_kernel(factor, *refs),
        out_shape=[one] * 4 + [jax.ShapeDtypeStruct((1, 900), F32), jax.ShapeDtypeStruct((1, 480), F32)],
        in_specs=[here] * 5,
        out_specs=[here] * 6,
        scratch_shapes=[pltpu.VMEM((96, 128), F32), pltpu.VMEM((8, 1280), F32)],
        name="tail",
    )(*outs, chunk)


def per_device(output_first_half, y_second, cot_first, cot_second, weight_space, temporal_weight):
    cells_all = (
        output_first_half.shape[0]
        * output_first_half.shape[1]
        * output_first_half.shape[2]
        * lax.axis_size("tm")
        * lax.axis_size("row")
    )
    factor = 1.0 / math.sqrt(cells_all)
    flat = [v.reshape(2, 64, 320) for v in (output_first_half, y_second, cot_first, cot_second)]
    *outs, chunk = block(*flat, weight_space, temporal_weight)
    *outs, space, time = tail(factor, outs, chunk)
    return tuple(v.reshape(output_first_half.shape) for v in outs) + (space.reshape(-1), time.reshape(-1))


def solution(mesh):
    in_specs = (
        P("tm", "row", None, None),
        P("tm", "row", None, None),
        P("tm", "row", None, None),
        P("tm", "row", None, None),
        P(),
        P(),
    )
    out_specs = (
        P("tm", "row", None, None),
        P("tm", "row", None, None),
        P("tm", "row", None, None),
        P("tm", "row", None, None),
        P(("tm", "row")),
        P(("tm", "row")),
    )
    return jax.shard_map(
        per_device, mesh=mesh, in_specs=in_specs, out_specs=out_specs, check_vma=False
    )
```

```python
import math

import jax
import jax.numpy as jnp
from jax import lax
from jax.experimental import pallas as pl
from jax.experimental.pallas import tpu as pltpu
from jax.sharding import PartitionSpec as P

MESH = pl.DeviceIdType.MESH
F32, BF16 = jnp.float32, jnp.bfloat16
HAAR = 0.7071067811865476
SHIFT, EARLY = 5, 2


def place():
    tm, row = lax.axis_index("tm"), lax.axis_index("row")
    return tm // 4, tm % 4, row // 4, (row // 2) % 2, row % 2


def ident(z, yl, x, yh, c):
    return (z * 4 + yl, x * 4 + yh * 2 + c)


def sigmoid(v):
    return 1.0 / (1.0 + jnp.exp(-v))


def slope(v):
    s = sigmoid(v)
    return s * (1.0 + v * (1.0 - s))


def dot(a, b, ca, cb):
    return lax.dot_general(a, b, (((ca,), (cb,)), ((), ())), preferred_element_type=F32)


def send(src, dst, snd, rcv, peer):
    return pltpu.make_async_remote_copy(
        src_ref=src, dst_ref=dst, send_sem=snd, recv_sem=rcv, device_id=peer, device_id_type=MESH
    )


def greet(z, yl, x, yh, c):
    tm, row = z * 4 + yl, x * 4 + yh * 2 + c
    peers = [((tm + 1) % 32, row), ((tm + 31) % 32, row), (tm, (row + 2 * c + 15) % 16)]
    for dx in range(4):
        for h in range(2):
            for dc in range(2):
                if (dx > 0) + h + dc == 1:
                    peers.append(ident(z, yl, (x + dx) % 4, (yh + h) % 2, (c + dc) % 2))
    for j in range(1, 4):
        for h in range(2):
            peers.append(ident(z, (yl + j) % 4, x, (yh + h) % 2, c))
    for d in range(1, 8):
        peers.append(ident((z + d) % 8, yl, x, yh, c))
    barrier = pltpu.get_barrier_semaphore()
    for peer in peers:
        pl.semaphore_signal(barrier, inc=1, device_id=peer, device_id_type=MESH)
    return barrier, len(peers)


def block_kernel(
    y1h, y2h, c1h, c2h, wsh, wth, xfh, xsh, gfh, gsh, out,
    xf, xs, gf, gs,    y1, y2, c1, c2, ws, wt, tb, hb, sq, cs, wide, pa, pg, rq, g, gt, rt, s0, r1, s1, r2, s2, r3, fin,
    in_sem, out_sem, t_snd, t_rcv, n_snd, n_rcv, r_snd, r_rcv, f_snd, f_rcv, q_snd, q_rcv, x_snd, x_rcv, y_snd, y_rcv, z_snd, z_rcv, g_snd, g_rcv,
):
    z, yl, x, yh, c = place()
    tm, row = z * 4 + yl, x * 4 + yh * 2 + c
    loads = [
        pltpu.make_async_copy(src, dst, in_sem.at[n])
        for n, (src, dst) in enumerate(((y1h, y1), (c2h, c2), (wth, wt), (y2h, y2), (c1h, c1), (wsh, ws)))
    ]
    for load in loads:
        load.start()
    stores = [pltpu.make_async_copy(src, dst, out_sem.at[n]) for n, (src, dst) in enumerate(((xf, xfh), (xs, xsh), (gf, gfh), (gs, gsh)))]
    barrier, met = greet(z, yl, x, yh, c)
    partner = ident(z, yl, x, yh, 1 - c)
    first_t, last_t = tm == 0, tm == 31
    own, other, far = 1 + c, 2 - c, 3 * c
    has_far = jnp.logical_not(jnp.logical_or(row == 0, row == 15))
    @pl.when(first_t)
    def _():
        tb[0] = jnp.zeros((2, 64, 640), BF16)

    @pl.when(last_t)
    def _():
        tb[2] = jnp.zeros((2, 64, 640), BF16)

    @pl.when(jnp.logical_not(has_far))
    def _():
        hb[far] = jnp.zeros((2, 5, 64, 128), BF16)

    ahead_t = [send(tb.at[1, n], tb.at[0, n], t_snd.at[n, 0], t_rcv.at[n, 0], ((tm + 1) % 32, row)) for n in range(2)]
    behind_t = [send(tb.at[1, n], tb.at[2, n], t_snd.at[n, 1], t_rcv.at[n, 1], ((tm + 31) % 32, row)) for n in range(2)]
    has_next, has_last = jnp.logical_not(last_t), jnp.logical_not(first_t)

    for n, ref in enumerate((y1, c2)):
        loads[n].wait()
        even, odd = ref[0].astype(F32), ref[1].astype(F32)
        sq[n, :, 0:320] = (even + odd) * HAAR
        sq[n, :, 320:640] = (even - odd) * HAAR
        v = sq[n]
        tb[1, n] = (v * sigmoid(v) if n == 0 else v).astype(BF16)
        if n == 0:
            pl.semaphore_wait(barrier, met)
        pl.when(has_next)(ahead_t[n].start)
        pl.when(has_last)(behind_t[n].start)

    pad = jnp.zeros((4, 2, 2, 8, 160), F32)
    for ref in (pa, pg):
        ref[:, :, :, 0:8] = pad
        ref[:, :, :, 72:80] = pad

    def time_taps(n, ks, q):
        at = pl.ds(q * 128, 128)
        both = None
        for k in ks:
            one = dot(tb[k, 0, :, at], wt[k, q], 1, 0) if n == 0 else dot(tb[2 - k, 1, :, at], wt[k, q], 1, 1)
            both = one if both is None else both + one
        return both

    def time_terms(ks):
        for k in ks:
            for q in range(5):
                at = pl.ds(q * 128, 128)
                gt[pl.ds((k * 5 + q) * 16, 16)] = dot(tb[1, 0, :, at], tb[2 - k, 1, :, at], 0, 0).reshape(16, 8, 128)

    loads[2].wait()
    for n in range(2):
        for q in range(5):
            cs[n, :, pl.ds(q * 128, 128)] = time_taps(n, (1,), q)
    time_terms((1,))
    loads[3].wait()
    loads[4].wait()
    far_row, near_row = [], []
    for n, (src, res) in enumerate(((y2, xs), (c1, gf))):
        pl.when(has_last)(ahead_t[n].wait_recv)
        pl.when(has_next)(behind_t[n].wait_recv)
        for q in range(5):
            at = pl.ds(q * 128, 128)
            whole = cs[n, :, at] + time_taps(n, (0, 2), q)
            cs[n, :, at] = whole if n == 0 else whole * slope(sq[0, :, at])
        low, high = cs[n, :, 0:320], cs[n, :, 320:640]
        for f in range(2):
            part = ((low + high if f == 0 else low - high) * HAAR).astype(BF16).astype(F32)
            new = (src[f].astype(F32) - part if n == 0 else src[f].astype(F32) + part).astype(BF16)
            res[f] = new
            held = new
            if n == 0:
                w = new.astype(F32)
                held = (w * sigmoid(w)).astype(BF16)
            hb[own, n, 2 * f] = held[:, 0:128]
            hb[own, n, 2 * f + 1] = held[:, 128:256]
            hb[own, n, 4, :, pl.ds(64 * f, 64)] = held[:, 256:320]
        far_row.append(send(hb.at[own, n], hb.at[3 - far, n], r_snd.at[n], r_rcv.at[n], (tm, (row + 2 * c + 15) % 16)))
        pl.when(has_far)(far_row[n].start)
        near_row.append(send(hb.at[own, n], hb.at[own, n], n_snd.at[n], n_rcv.at[n], partner))
        near_row[n].start()
        stores[1 + n].start()

    time_terms((0, 2))

    def pack_time(n, carry):
        chunk = (n // 4 + 8 - SHIFT) % 8 * 4 + n % 4
        tiles = gt[pl.ds((15 * chunk) // 2, 8)].astype(BF16)

        def put(ref, m):
            ref[m, n % 4, n // 4] = tiles[0:3]
            ref[m + 1, n % 4, n // 4] = tiles[3:6]
            ref[m + 2, n % 4, n // 4, 0:2] = tiles[6:8]
            ref[m + 2, n % 4, n // 4, 2:3] = jnp.zeros((1, 8, 128), BF16)

        pl.when(c == 0)(lambda: put(rt, 0))
        pl.when(c == 1)(lambda: put(s0, 1))
        return carry

    lax.fori_loop(0, 32, pack_time, 0)
    time_half = [send(rt.at[xp - 1], rt.at[xp - 1], q_snd.at[xp - 1], q_rcv.at[xp - 1], partner) for xp in (1, 2, 3)]

    @pl.when(c == 0)
    def _():
        for copy in time_half:
            copy.start()

    def widen(slot, n):
        for f in range(2):
            at = pl.ds(f * 64, 64)
            wide[n, at, 0:128] = hb[slot, n, 2 * f].astype(F32)
            wide[n, at, 128:256] = hb[slot, n, 2 * f + 1].astype(F32)
            wide[n, at, 256:320] = hb[slot, n, 4, :, pl.ds(64 * f, 64)].astype(F32)

    def spread(slot, n):
        widen(slot, n)
        for q in range(2):
            (pa, pg)[n][slot, q, :, 8:72] = wide[n, :, pl.ds(q * 160, 160)].reshape(2, 64, 160)

    def right_side(slot):
        for q in range(2):
            for n in range(4):
                rq[q, slot - 1, :, pl.ds(32 * n, 32)] = jnp.where(
                    c == 0, wide[1, :, pl.ds(q * 160 + 32 * n, 32)], wide[1, :, pl.ds(q * 160 + 128, 32)]
                ).astype(BF16)

    for slot in (own, other):
        for n in range(2):
            if slot is other:
                near_row[n].wait_recv()
            spread(slot, n)
        right_side(slot)

    def left(slot, b, q):
        return pa[slot, q, :, pl.ds(7 + b, 64)].reshape(128, 160).astype(BF16)

    def space_terms(rows):
        for q in range(2):
            for a in rows:
                for b in range(3):
                    tap = a * 3 + b
                    both = jnp.concatenate([left(a, b, q), left(a + 1, b, q)], axis=0)
                    g[pl.ds((tap * 2 + q) * 20, 20)] = dot(both, rq[q].reshape(256, 128), 0, 0).reshape(20, 8, 128)

    lane = lax.broadcasted_iota(jnp.int32, (3, 8, 128), 2)

    def pack_space(lo, count):
        def pack(n, carry):
            zz, yp = lo + n // 4, n % 4
            chunk = (zz + 8 - SHIFT) % 8 * 4 + yp
            tiles = g[pl.ds((45 * chunk) // 4, 12)]

            @pl.when(c == 0)
            def _():
                for m in range(4):
                    s0[m, yp, zz] = tiles[3 * m : 3 * m + 3].astype(BF16)

            @pl.when(c == 1)
            def _():
                one, two = jnp.where(lane < 32, tiles[0:3], tiles[3:6]), jnp.where(lane < 96, tiles[6:9], tiles[9:12])
                s0[0, yp, zz] = jnp.where(lane < 64, one, two).astype(BF16)

            return carry

        lax.fori_loop(0, count * 4, pack, 0)

    def group(xp, yp):
        return (xp + 4 - yp) % 4

    def along_x(k, j, part):
        xp, yp = (x + k) % 4, (yl + j) % 4
        at = pl.ds(0, EARLY) if isinstance(part, int) and part == 0 else pl.ds(EARLY + 3 * (part - 1), 3)
        return send(s0.at[group(xp, yp), yp, at], r1.at[k - 1, yp, at], x_snd.at[k - 1, j, part], x_rcv.at[k - 1, j, part], ident(z, yl, xp, yh, c))

    space_terms((1,))

    @pl.when(c == 1)
    def _():
        for xp in (1, 2, 3):
            time_half[xp - 1].wait_recv()
            for yp in range(4):
                s0[xp, yp] = (s0[xp, yp].astype(F32) + rt[xp - 1, yp].astype(F32)).astype(BF16)

    pack_space(0, EARLY)
    order = [(k, j) for j in (1, 2, 3, 0) for k in (2, 1, 3)]
    timed = {(k, j): jnp.logical_and(c == 1, group((x + k) % 4, (yl + j) % 4) != 0) for k, j in order}
    for k, j in order:
        along_x(k, j, 0).start()

        @pl.when(timed[k, j])
        def _():
            along_x(k, j, 1).start()
            along_x(k, j, 2).start()

    def late_part(part):
        pack_space(EARLY + 3 * (part - 1), 3)
        for k, j in order:
            pl.when(jnp.logical_not(timed[k, j]))(along_x(k, j, part).start)


    pl.when(has_far)(far_row[0].wait_recv)
    pass_on = send(hb.at[far, 0], hb.at[far, 0], f_snd.at[0], f_rcv.at[0], partner)
    pass_on.start()
    spread(far, 0)
    space_terms((2 * c,))
    late_part(2 - c)
    pass_on.wait_recv()
    spread(3 - far, 0)
    space_terms((2 - 2 * c,))
    late_part(1 + c)

    def along_y(j, h):
        yp, hp = (yl + j) % 4, (yh + h) % 2
        return send(s1.at[yp, pl.ds(hp * 4, 4)], r2.at[2 * j + h], y_snd.at[2 * j + h], y_rcv.at[2 * j + h], ident(z, yp, x, hp, c))

    def sum_x(j):
        yp = (yl + j) % 4
        for k in (1, 2, 3):
            for part in range(3):
                along_x(k, j, part).wait_recv()
        total = s0[group(x, yp), yp].astype(F32)
        for k in (1, 2, 3):
            total += r1[k - 1, yp].astype(F32)
        s1[yp] = total.astype(BF16)
        for h in (1, 0):
            if j or h:
                along_y(j, h).start()

    for early in (True, False):
        for j in (1, 2, 3, 0):
            is_time = jnp.logical_and(c == 1, group(x, (yl + j) % 4) != 0)
            pl.when(is_time if early else jnp.logical_not(is_time))(lambda j=j: sum_x(j))

    total = s1[yl, pl.ds(yh * 4, 4)].astype(F32)
    others = [(j, h) for j in (1, 2, 3, 0) for h in (1, 0) if j or h]
    for j, h in others:
        along_y(j, h).wait_recv()
    for j, h in others:
        total += r2[2 * j + h].astype(F32)
    s2[...] = total.astype(BF16)

    mine = (z + SHIFT) % 8 // 4 == yh

    def along_z(d, finish):
        zp = (z + d) % 8
        zz = (zp + SHIFT) % 8
        copy = send(s2.at[zz % 4], r3.at[d - 1], z_snd.at[d - 1], z_rcv.at[d - 1], ident(zp, yl, x, yh, c))
        pl.when(zz // 4 == yh)(copy.wait_send if finish else copy.start)

    def takes(slot, to):
        space, time = 90 * tm % 8 + 900 * to // 160, 60 * tm % 8 + 480 * to // 128
        low = 24 * (slot % 5)
        main = jnp.logical_and(space <= low + 23, space + 6 >= low)
        late = jnp.logical_and(time <= low + 23, time + 4 >= low)
        return jnp.logical_or(slot == 4, jnp.logical_or(jnp.logical_and(slot < 4, main), jnp.logical_and(slot > 4, late)))

    offsets = [(dx, h, dc) for dx in (2, 1, 3, 0) for h in (1, 0) for dc in (1, 0) if dx or h or dc]

    def over_row(finish):
        slot = c * 4 + group(x, yl)
        for dx, h, dc in offsets:
            n, xp, hp, cp = dx * 2 + dc, (x + dx) % 4, (yh + h) % 2, (c + dc) % 2
            copy = send(fin.at[slot], fin.at[slot], g_snd.at[n, h], g_rcv.at[n], ident(z, yl, xp, hp, cp))
            pl.when(takes(slot, xp * 4 + hp * 2 + cp))(copy.wait_send if finish else copy.start)

    for d in range(1, 8):
        along_z(d, False)

    pl.when(has_far)(far_row[1].wait_recv)
    spread(far, 1)
    loads[5].wait()
    for q in range(2):
        ahead, back = None, None
        for a in range(3):
            for b in range(3):
                one = dot(left(c + a, b, q), ws[a, b, q], 1, 0)
                moved = pg[c + 2 - a, q, :, pl.ds(9 - b, 64)].reshape(128, 160).astype(BF16)
                two = dot(moved, ws[a, b, q], 1, 1)
                ahead, back = (one, two) if ahead is None else (ahead + one, back + two)
        wide[0, :, pl.ds(q * 160, 160)] = ahead
        wide[1, :, pl.ds(q * 160, 160)] = back
    for f in range(2):
        at = pl.ds(f * 64, 64)
        xf[f] = (y1[f].astype(F32) - wide[0, at]).astype(BF16)
        gs[f] = (c2[f].astype(F32) + wide[1, at] * slope(xs[f].astype(F32))).astype(BF16)
    stores[0].start()
    stores[3].start()

    @pl.when(mine)
    def _():
        for d in range(1, 8):
            send(s2.at[0], r3.at[d - 1], z_snd.at[d - 1], z_rcv.at[d - 1], ident((z + d) % 8, yl, x, yh, c)).wait_recv()
        last = s2[(z + SHIFT) % 4].astype(F32)
        for d in range(1, 8):
            last += r3[d - 1].astype(F32)
        fin[c * 4 + group(x, yl)] = last
        over_row(False)

    for store in stores:
        store.wait()
    for n in range(2):
        pl.when(has_next)(ahead_t[n].wait_send)
        pl.when(has_last)(behind_t[n].wait_send)
        pl.when(has_far)(far_row[n].wait_send)
        near_row[n].wait_send()
    pass_on.wait_send()

    @pl.when(c == 0)
    def _():
        for copy in time_half:
            copy.wait_send()

    for k in (1, 2, 3):
        for j in range(4):
            for part in range(3):
                along_x(k, j, part).wait_send()
    for j, h in others:
        along_y(j, h).wait_send()
    for d in range(1, 8):
        along_z(d, True)

    for dx in range(4):
        for dc in range(2):
            n = dx * 2 + dc
            src = (c + dc) % 2 * 4 + group((x + 4 - dx) % 4, yl)
            copy = send(fin.at[src], fin.at[src], g_snd.at[n, 1], g_rcv.at[n], ident(z, yl, (x + dx) % 4, 1 - yh, (c + dc) % 2))
            wanted = takes(src, row)
            pl.when(wanted if n else jnp.logical_and(wanted, jnp.logical_not(mine)))(copy.wait_recv)
    out[...] = fin[...]
    pl.when(mine)(lambda: over_row(True))


def block(y1, y2, c1, c2, ws, wt):
    dma = pltpu.SemaphoreType.DMA
    here, there = pl.BlockSpec(memory_space=pltpu.VMEM), pl.BlockSpec(memory_space=pl.ANY)
    one = jax.ShapeDtypeStruct((2, 64, 320), BF16)
    vm = pltpu.VMEM
    return pl.pallas_call(
        block_kernel,
        out_shape=[one] * 4 + [jax.ShapeDtypeStruct((8, 3, 8, 128), F32)],
        in_specs=[there] * 6,
        out_specs=[there] * 4 + [here],
        scratch_shapes=[vm((2, 64, 320), BF16)] * 8
        + [
            vm((3, 3, 2, 160, 160), BF16),
            vm((3, 5, 128, 128), BF16),
            vm((3, 2, 64, 640), BF16),
            vm((4, 2, 5, 64, 128), BF16),
            vm((2, 64, 640), F32),
            vm((2, 64, 640), F32),
            vm((2, 128, 320), F32),
            vm((4, 2, 2, 80, 160), F32),
            vm((4, 2, 2, 80, 160), F32),
            vm((2, 2, 128, 128), BF16),
            vm((360, 8, 128), F32),
            vm((240, 8, 128), F32),
            vm((3, 4, 8, 3, 8, 128), BF16),
            vm((4, 4, 8, 3, 8, 128), BF16),
            vm((3, 4, 8, 3, 8, 128), BF16),
            vm((4, 8, 3, 8, 128), BF16),
            vm((8, 4, 3, 8, 128), BF16),
            vm((4, 3, 8, 128), BF16),
            vm((7, 3, 8, 128), BF16),
            vm((8, 3, 8, 128), F32),
        ]
        + [dma((6,)), dma((4,))]
        + [dma((2, 2))] * 2
        + [dma((2,))] * 4
        + [dma((1,))] * 2
        + [dma((3,))] * 2
        + [dma((3, 4, 3))] * 2
        + [dma((8,))] * 2
        + [dma((7,))] * 2
        + [dma((8, 2)), dma((8,))],
        compiler_params=pltpu.CompilerParams(collective_id=5, has_side_effects=True, vmem_limit_bytes=60 * 1024 * 1024),
        name="block",
    )(y1, y2, c1, c2, ws, wt)


def tail_kernel(factor, xf, xs, gf, gs, chunk, xf_o, xs_o, gf_o, gs_o, space, time, rest, line):
    tm, row = lax.axis_index("tm"), lax.axis_index("row")
    for src, dst in ((xf, xf_o), (xs, xs_o), (gf, gf_o), (gs, gs_o)):
        dst[...] = src[...]
    four = chunk[4].reshape(24, 128)
    for n in range(4):
        rest[pl.ds(24 * n, 24), 0:32] = four[:, 32 * n : 32 * n + 32]
    flat = 900 * row
    start = 90 * tm % 8 + flat // 160
    main = pltpu.roll(chunk[0:4].reshape(96, 128), (96 - start) % 96, 0)
    side = pltpu.roll(rest[...], (96 - start) % 96, 0)
    for n in range(7):
        line[0:1, pl.ds(160 * n, 128)] = main[n : n + 1]
        line[0:1, pl.ds(160 * n + 128, 32)] = side[n : n + 1, 0:32]
    space[...] = pltpu.roll(line[...], (1280 - flat % 160) % 1280, 1)[0:1, 0:900] * factor
    flat = 480 * row
    start = 60 * tm % 8 + flat // 128
    main = pltpu.roll(chunk[5:8].reshape(72, 128), (72 - start) % 72, 0)
    for n in range(5):
        line[0:1, pl.ds(128 * n, 128)] = main[n : n + 1]
    time[...] = pltpu.roll(line[...], (1280 - flat % 128) % 1280, 1)[0:1, 0:480] * factor


def tail(factor, outs, chunk):
    here = pl.BlockSpec(memory_space=pltpu.VMEM)
    one = jax.ShapeDtypeStruct((2, 64, 320), BF16)
    return pl.pallas_call(
        lambda *refs: tail_kernel(factor, *refs),
        out_shape=[one] * 4 + [jax.ShapeDtypeStruct((1, 900), F32), jax.ShapeDtypeStruct((1, 480), F32)],
        in_specs=[here] * 5,
        out_specs=[here] * 6,
        scratch_shapes=[pltpu.VMEM((96, 128), F32), pltpu.VMEM((8, 1280), F32)],
        name="tail",
    )(*outs, chunk)


def per_device(output_first_half, y_second, cot_first, cot_second, weight_space, temporal_weight):
    cells_all = (
        output_first_half.shape[0]
        * output_first_half.shape[1]
        * output_first_half.shape[2]
        * lax.axis_size("tm")
        * lax.axis_size("row")
    )
    factor = 1.0 / math.sqrt(cells_all)
    flat = [v.reshape(2, 64, 320) for v in (output_first_half, y_second, cot_first, cot_second)]
    *outs, chunk = block(*flat, weight_space, temporal_weight)
    *outs, space, time = tail(factor, outs, chunk)
    return tuple(v.reshape(output_first_half.shape) for v in outs) + (space.reshape(-1), time.reshape(-1))


def solution(mesh):
    in_specs = (
        P("tm", "row", None, None),
        P("tm", "row", None, None),
        P("tm", "row", None, None),
        P("tm", "row", None, None),
        P(),
        P(),
    )
    out_specs = (
        P("tm", "row", None, None),
        P("tm", "row", None, None),
        P("tm", "row", None, None),
        P("tm", "row", None, None),
        P(("tm", "row")),
        P(("tm", "row")),
    )
    return jax.shard_map(
        per_device, mesh=mesh, in_specs=in_specs, out_specs=out_specs, check_vma=False
    )
```

```python
import math

import jax
import jax.numpy as jnp
from jax import lax
from jax.experimental import pallas as pl
from jax.experimental.pallas import tpu as pltpu
from jax.sharding import PartitionSpec as P

MESH = pl.DeviceIdType.MESH
F32, BF16 = jnp.float32, jnp.bfloat16
HAAR = 0.7071067811865476
SHIFT, EARLY = 5, 2


def place():
    tm, row = lax.axis_index("tm"), lax.axis_index("row")
    return tm // 4, tm % 4, row // 4, (row // 2) % 2, row % 2


def ident(z, yl, x, yh, c):
    return (z * 4 + yl, x * 4 + yh * 2 + c)


def sigmoid(v):
    return 1.0 / (1.0 + jnp.exp(-v))


def slope(v):
    s = sigmoid(v)
    return s * (1.0 + v * (1.0 - s))


def dot(a, b, ca, cb):
    return lax.dot_general(a, b, (((ca,), (cb,)), ((), ())), preferred_element_type=F32)


def send(src, dst, snd, rcv, peer):
    return pltpu.make_async_remote_copy(
        src_ref=src, dst_ref=dst, send_sem=snd, recv_sem=rcv, device_id=peer, device_id_type=MESH
    )


def greet(z, yl, x, yh, c):
    tm, row = z * 4 + yl, x * 4 + yh * 2 + c
    peers = [((tm + 1) % 32, row), ((tm + 31) % 32, row), (tm, (row + 2 * c + 15) % 16)]
    for dx in range(4):
        for h in range(2):
            for dc in range(2):
                if (dx > 0) + h + dc == 1:
                    peers.append(ident(z, yl, (x + dx) % 4, (yh + h) % 2, (c + dc) % 2))
    for j in range(1, 4):
        for h in range(2):
            peers.append(ident(z, (yl + j) % 4, x, (yh + h) % 2, c))
    for d in range(1, 8):
        peers.append(ident((z + d) % 8, yl, x, yh, c))
    barrier = pltpu.get_barrier_semaphore()
    for peer in peers:
        pl.semaphore_signal(barrier, inc=1, device_id=peer, device_id_type=MESH)
    return barrier, len(peers)


def block_kernel(
    y1h, y2h, c1h, c2h, wsh, wth, xfh, xsh, gfh, gsh, out,
    xf, xs, gf, gs,    y1, y2, c1, c2, ws, wt, tb, hb, sq, cs, wide, pa, pg, rq, g, gt, rt, s0, r1, s1, r2, s2, r3, fin,
    in_sem, out_sem, t_snd, t_rcv, n_snd, n_rcv, r_snd, r_rcv, f_snd, f_rcv, q_snd, q_rcv, x_snd, x_rcv, y_snd, y_rcv, z_snd, z_rcv, g_snd, g_rcv,
):
    z, yl, x, yh, c = place()
    tm, row = z * 4 + yl, x * 4 + yh * 2 + c
    loads = [
        pltpu.make_async_copy(src, dst, in_sem.at[n])
        for n, (src, dst) in enumerate(((y1h, y1), (c2h, c2), (wth, wt), (y2h, y2), (c1h, c1), (wsh, ws)))
    ]
    for load in loads:
        load.start()
    stores = [pltpu.make_async_copy(src, dst, out_sem.at[n]) for n, (src, dst) in enumerate(((xf, xfh), (xs, xsh), (gf, gfh), (gs, gsh)))]
    barrier, met = greet(z, yl, x, yh, c)
    partner = ident(z, yl, x, yh, 1 - c)
    first_t, last_t = tm == 0, tm == 31
    own, other, far = 1 + c, 2 - c, 3 * c
    has_far = jnp.logical_not(jnp.logical_or(row == 0, row == 15))
    @pl.when(first_t)
    def _():
        tb[0] = jnp.zeros((2, 64, 640), BF16)

    @pl.when(last_t)
    def _():
        tb[2] = jnp.zeros((2, 64, 640), BF16)

    @pl.when(jnp.logical_not(has_far))
    def _():
        hb[far] = jnp.zeros((2, 5, 64, 128), BF16)

    ahead_t = [send(tb.at[1, n], tb.at[0, n], t_snd.at[n, 0], t_rcv.at[n, 0], ((tm + 1) % 32, row)) for n in range(2)]
    behind_t = [send(tb.at[1, n], tb.at[2, n], t_snd.at[n, 1], t_rcv.at[n, 1], ((tm + 31) % 32, row)) for n in range(2)]
    has_next, has_last = jnp.logical_not(last_t), jnp.logical_not(first_t)

    for n, ref in enumerate((y1, c2)):
        loads[n].wait()
        even, odd = ref[0].astype(F32), ref[1].astype(F32)
        sq[n, :, 0:320] = (even + odd) * HAAR
        sq[n, :, 320:640] = (even - odd) * HAAR
        v = sq[n]
        tb[1, n] = (v * sigmoid(v) if n == 0 else v).astype(BF16)
        if n == 0:
            pl.semaphore_wait(barrier, met)
        pl.when(has_next)(ahead_t[n].start)
        pl.when(has_last)(behind_t[n].start)

    pad = jnp.zeros((4, 2, 2, 8, 160), F32)
    for ref in (pa, pg):
        ref[:, :, :, 0:8] = pad
        ref[:, :, :, 72:80] = pad

    def time_taps(n, ks, q):
        at = pl.ds(q * 128, 128)
        both = None
        for k in ks:
            one = dot(tb[k, 0, :, at], wt[k, q], 1, 0) if n == 0 else dot(tb[2 - k, 1, :, at], wt[k, q], 1, 1)
            both = one if both is None else both + one
        return both

    def time_terms(ks):
        for k in ks:
            for q in range(5):
                at = pl.ds(q * 128, 128)
                gt[pl.ds((k * 5 + q) * 16, 16)] = dot(tb[1, 0, :, at], tb[2 - k, 1, :, at], 0, 0).reshape(16, 8, 128)

    loads[2].wait()
    for n in range(2):
        for q in range(5):
            cs[n, :, pl.ds(q * 128, 128)] = time_taps(n, (1,), q)
    time_terms((1,))
    loads[3].wait()
    loads[4].wait()
    far_row, near_row = [], []
    for n, (src, res) in enumerate(((y2, xs), (c1, gf))):
        pl.when(has_last)(ahead_t[n].wait_recv)
        pl.when(has_next)(behind_t[n].wait_recv)
        for q in range(5):
            at = pl.ds(q * 128, 128)
            whole = cs[n, :, at] + time_taps(n, (0, 2), q)
            cs[n, :, at] = whole if n == 0 else whole * slope(sq[0, :, at])
        low, high = cs[n, :, 0:320], cs[n, :, 320:640]
        for f in range(2):
            part = ((low + high if f == 0 else low - high) * HAAR).astype(BF16).astype(F32)
            new = (src[f].astype(F32) - part if n == 0 else src[f].astype(F32) + part).astype(BF16)
            res[f] = new
            held = new
            if n == 0:
                w = new.astype(F32)
                held = (w * sigmoid(w)).astype(BF16)
            hb[own, n, 2 * f] = held[:, 0:128]
            hb[own, n, 2 * f + 1] = held[:, 128:256]
            hb[own, n, 4, :, pl.ds(64 * f, 64)] = held[:, 256:320]
        far_row.append(send(hb.at[own, n], hb.at[3 - far, n], r_snd.at[n], r_rcv.at[n], (tm, (row + 2 * c + 15) % 16)))
        pl.when(has_far)(far_row[n].start)
        near_row.append(send(hb.at[own, n], hb.at[own, n], n_snd.at[n], n_rcv.at[n], partner))
        near_row[n].start()
        stores[1 + n].start()

    time_terms((0, 2))

    def pack_time(n, carry):
        chunk = (n // 4 + 8 - SHIFT) % 8 * 4 + n % 4
        tiles = gt[pl.ds((15 * chunk) // 2, 8)].astype(BF16)

        def put(ref, m):
            ref[m, n % 4, n // 4] = tiles[0:3]
            ref[m + 1, n % 4, n // 4] = tiles[3:6]
            ref[m + 2, n % 4, n // 4, 0:2] = tiles[6:8]
            ref[m + 2, n % 4, n // 4, 2:3] = jnp.zeros((1, 8, 128), BF16)

        pl.when(c == 0)(lambda: put(rt, 0))
        pl.when(c == 1)(lambda: put(s0, 1))
        return carry

    lax.fori_loop(0, 32, pack_time, 0)
    time_half = [send(rt.at[xp - 1], rt.at[xp - 1], q_snd.at[xp - 1], q_rcv.at[xp - 1], partner) for xp in (1, 2, 3)]

    @pl.when(c == 0)
    def _():
        for copy in time_half:
            copy.start()

    def widen(slot, n):
        for f in range(2):
            at = pl.ds(f * 64, 64)
            wide[n, at, 0:128] = hb[slot, n, 2 * f].astype(F32)
            wide[n, at, 128:256] = hb[slot, n, 2 * f + 1].astype(F32)
            wide[n, at, 256:320] = hb[slot, n, 4, :, pl.ds(64 * f, 64)].astype(F32)

    def spread(slot, n):
        widen(slot, n)
        for q in range(2):
            (pa, pg)[n][slot, q, :, 8:72] = wide[n, :, pl.ds(q * 160, 160)].reshape(2, 64, 160)

    def right_side(slot):
        for q in range(2):
            for n in range(4):
                rq[q, slot - 1, :, pl.ds(32 * n, 32)] = jnp.where(
                    c == 0, wide[1, :, pl.ds(q * 160 + 32 * n, 32)], wide[1, :, pl.ds(q * 160 + 128, 32)]
                ).astype(BF16)

    for slot in (own, other):
        for n in range(2):
            if slot is other:
                near_row[n].wait_recv()
            spread(slot, n)
        right_side(slot)

    def left(slot, b, q):
        return pa[slot, q, :, pl.ds(7 + b, 64)].reshape(128, 160).astype(BF16)

    def space_terms(rows):
        for q in range(2):
            for a in rows:
                for b in range(3):
                    tap = a * 3 + b
                    both = jnp.concatenate([left(a, b, q), left(a + 1, b, q)], axis=0)
                    g[pl.ds((tap * 2 + q) * 20, 20)] = dot(both, rq[q].reshape(256, 128), 0, 0).reshape(20, 8, 128)

    lane = lax.broadcasted_iota(jnp.int32, (3, 8, 128), 2)

    def pack_space(lo, count):
        def pack(n, carry):
            zz, yp = lo + n // 4, n % 4
            chunk = (zz + 8 - SHIFT) % 8 * 4 + yp
            tiles = g[pl.ds((45 * chunk) // 4, 12)]

            @pl.when(c == 0)
            def _():
                for m in range(4):
                    s0[m, yp, zz] = tiles[3 * m : 3 * m + 3].astype(BF16)

            @pl.when(c == 1)
            def _():
                one, two = jnp.where(lane < 32, tiles[0:3], tiles[3:6]), jnp.where(lane < 96, tiles[6:9], tiles[9:12])
                s0[0, yp, zz] = jnp.where(lane < 64, one, two).astype(BF16)

            return carry

        lax.fori_loop(0, count * 4, pack, 0)

    def group(xp, yp):
        return (xp + 4 - yp) % 4

    def along_x(k, j, part):
        xp, yp = (x + k) % 4, (yl + j) % 4
        at = pl.ds(0, EARLY) if isinstance(part, int) and part == 0 else pl.ds(EARLY + 3 * (part - 1), 3)
        return send(s0.at[group(xp, yp), yp, at], r1.at[k - 1, yp, at], x_snd.at[k - 1, j, part], x_rcv.at[k - 1, j, part], ident(z, yl, xp, yh, c))

    space_terms((1,))

    @pl.when(c == 1)
    def _():
        for xp in (1, 2, 3):
            time_half[xp - 1].wait_recv()
            for yp in range(4):
                s0[xp, yp] = (s0[xp, yp].astype(F32) + rt[xp - 1, yp].astype(F32)).astype(BF16)

    pack_space(0, EARLY)
    order = [(k, j) for j in (1, 2, 3, 0) for k in (2, 1, 3)]
    timed = {(k, j): jnp.logical_and(c == 1, group((x + k) % 4, (yl + j) % 4) != 0) for k, j in order}
    for k, j in order:
        along_x(k, j, 0).start()

        @pl.when(timed[k, j])
        def _():
            along_x(k, j, 1).start()
            along_x(k, j, 2).start()

    def late_part(part):
        pack_space(EARLY + 3 * (part - 1), 3)
        for k, j in order:
            pl.when(jnp.logical_not(timed[k, j]))(along_x(k, j, part).start)


    pl.when(has_far)(far_row[0].wait_recv)
    pass_on = send(hb.at[far, 0], hb.at[far, 0], f_snd.at[0], f_rcv.at[0], partner)
    pass_on.start()
    spread(far, 0)
    space_terms((2 * c,))
    late_part(2 - c)
    pass_on.wait_recv()
    spread(3 - far, 0)
    space_terms((2 - 2 * c,))
    late_part(1 + c)

    def along_y(j, h):
        yp, hp = (yl + j) % 4, (yh + h) % 2
        return send(s1.at[yp, pl.ds(hp * 4, 4)], r2.at[2 * j + h], y_snd.at[2 * j + h], y_rcv.at[2 * j + h], ident(z, yp, x, hp, c))

    def sum_x(j):
        yp = (yl + j) % 4
        for k in (1, 2, 3):
            for part in range(3):
                along_x(k, j, part).wait_recv()
        total = s0[group(x, yp), yp].astype(F32)
        for k in (1, 2, 3):
            total += r1[k - 1, yp].astype(F32)
        s1[yp] = total.astype(BF16)
        for h in (1, 0):
            if j or h:
                along_y(j, h).start()

    for early in (True, False):
        for j in (1, 2, 3, 0):
            is_time = jnp.logical_and(c == 1, group(x, (yl + j) % 4) != 0)
            pl.when(is_time if early else jnp.logical_not(is_time))(lambda j=j: sum_x(j))

    total = s1[yl, pl.ds(yh * 4, 4)].astype(F32)
    others = [(j, h) for j in (1, 2, 3, 0) for h in (1, 0) if j or h]
    for j, h in others:
        along_y(j, h).wait_recv()
    for j, h in others:
        total += r2[2 * j + h].astype(F32)
    s2[...] = total.astype(BF16)

    mine = (z + SHIFT) % 8 // 4 == yh

    def along_z(d, finish):
        zp = (z + d) % 8
        zz = (zp + SHIFT) % 8
        copy = send(s2.at[zz % 4], r3.at[d - 1], z_snd.at[d - 1], z_rcv.at[d - 1], ident(zp, yl, x, yh, c))
        pl.when(zz // 4 == yh)(copy.wait_send if finish else copy.start)

    def takes(slot, to, t):
        space, time = 90 * tm % 8 + 900 * to // 160, 60 * tm % 8 + 480 * to // 128

        def meets(start, count, low):
            return jnp.logical_and(start <= low + 7, start + count - 1 >= low)

        low = 24 * (slot % 5) + 8 * t
        rest = meets(space, 7, 8 * t)
        for n in range(1, 4):
            rest = jnp.logical_or(rest, meets(space, 7, 24 * n + 8 * t))
        main = jnp.logical_and(slot < 4, meets(space, 7, low))
        late = jnp.logical_and(slot > 4, meets(time, 5, low))
        return jnp.logical_or(jnp.logical_and(slot == 4, rest), jnp.logical_or(main, late))

    offsets = [(dx, h, dc) for dx in (2, 1, 3, 0) for h in (1, 0) for dc in (1, 0) if dx or h or dc]

    def over_row(finish):
        slot = c * 4 + group(x, yl)
        for dx, h, dc in offsets:
            n, xp, hp, cp = dx * 2 + dc, (x + dx) % 4, (yh + h) % 2, (c + dc) % 2
            for t in range(3):
                copy = send(fin.at[slot, t], fin.at[slot, t], g_snd.at[n, h, t], g_rcv.at[n, t], ident(z, yl, xp, hp, cp))
                pl.when(takes(slot, xp * 4 + hp * 2 + cp, t))(copy.wait_send if finish else copy.start)

    for d in range(1, 8):
        along_z(d, False)

    pl.when(has_far)(far_row[1].wait_recv)
    spread(far, 1)
    loads[5].wait()
    for q in range(2):
        ahead, back = None, None
        for a in range(3):
            for b in range(3):
                one = dot(left(c + a, b, q), ws[a, b, q], 1, 0)
                moved = pg[c + 2 - a, q, :, pl.ds(9 - b, 64)].reshape(128, 160).astype(BF16)
                two = dot(moved, ws[a, b, q], 1, 1)
                ahead, back = (one, two) if ahead is None else (ahead + one, back + two)
        wide[0, :, pl.ds(q * 160, 160)] = ahead
        wide[1, :, pl.ds(q * 160, 160)] = back
    for f in range(2):
        at = pl.ds(f * 64, 64)
        xf[f] = (y1[f].astype(F32) - wide[0, at]).astype(BF16)
        gs[f] = (c2[f].astype(F32) + wide[1, at] * slope(xs[f].astype(F32))).astype(BF16)
    stores[0].start()
    stores[3].start()

    @pl.when(mine)
    def _():
        for d in range(1, 8):
            send(s2.at[0], r3.at[d - 1], z_snd.at[d - 1], z_rcv.at[d - 1], ident((z + d) % 8, yl, x, yh, c)).wait_recv()
        last = s2[(z + SHIFT) % 4].astype(F32)
        for d in range(1, 8):
            last += r3[d - 1].astype(F32)
        fin[c * 4 + group(x, yl)] = last
        over_row(False)

    for store in stores:
        store.wait()
    for n in range(2):
        pl.when(has_next)(ahead_t[n].wait_send)
        pl.when(has_last)(behind_t[n].wait_send)
        pl.when(has_far)(far_row[n].wait_send)
        near_row[n].wait_send()
    pass_on.wait_send()

    @pl.when(c == 0)
    def _():
        for copy in time_half:
            copy.wait_send()

    for k in (1, 2, 3):
        for j in range(4):
            for part in range(3):
                along_x(k, j, part).wait_send()
    for j, h in others:
        along_y(j, h).wait_send()
    for d in range(1, 8):
        along_z(d, True)

    for dx in range(4):
        for dc in range(2):
            n = dx * 2 + dc
            src = (c + dc) % 2 * 4 + group((x + 4 - dx) % 4, yl)
            for t in range(3):
                copy = send(fin.at[src, t], fin.at[src, t], g_snd.at[n, 1, t], g_rcv.at[n, t], ident(z, yl, (x + dx) % 4, 1 - yh, (c + dc) % 2))
                wanted = takes(src, row, t)
                pl.when(wanted if n else jnp.logical_and(wanted, jnp.logical_not(mine)))(copy.wait_recv)
    out[...] = fin[...]
    pl.when(mine)(lambda: over_row(True))


def block(y1, y2, c1, c2, ws, wt):
    dma = pltpu.SemaphoreType.DMA
    here, there = pl.BlockSpec(memory_space=pltpu.VMEM), pl.BlockSpec(memory_space=pl.ANY)
    one = jax.ShapeDtypeStruct((2, 64, 320), BF16)
    vm = pltpu.VMEM
    return pl.pallas_call(
        block_kernel,
        out_shape=[one] * 4 + [jax.ShapeDtypeStruct((8, 3, 8, 128), F32)],
        in_specs=[there] * 6,
        out_specs=[there] * 4 + [here],
        scratch_shapes=[vm((2, 64, 320), BF16)] * 8
        + [
            vm((3, 3, 2, 160, 160), BF16),
            vm((3, 5, 128, 128), BF16),
            vm((3, 2, 64, 640), BF16),
            vm((4, 2, 5, 64, 128), BF16),
            vm((2, 64, 640), F32),
            vm((2, 64, 640), F32),
            vm((2, 128, 320), F32),
            vm((4, 2, 2, 80, 160), F32),
            vm((4, 2, 2, 80, 160), F32),
            vm((2, 2, 128, 128), BF16),
            vm((360, 8, 128), F32),
            vm((240, 8, 128), F32),
            vm((3, 4, 8, 3, 8, 128), BF16),
            vm((4, 4, 8, 3, 8, 128), BF16),
            vm((3, 4, 8, 3, 8, 128), BF16),
            vm((4, 8, 3, 8, 128), BF16),
            vm((8, 4, 3, 8, 128), BF16),
            vm((4, 3, 8, 128), BF16),
            vm((7, 3, 8, 128), BF16),
            vm((8, 3, 8, 128), F32),
        ]
        + [dma((6,)), dma((4,))]
        + [dma((2, 2))] * 2
        + [dma((2,))] * 4
        + [dma((1,))] * 2
        + [dma((3,))] * 2
        + [dma((3, 4, 3))] * 2
        + [dma((8,))] * 2
        + [dma((7,))] * 2
        + [dma((8, 2, 3)), dma((8, 3))],
        compiler_params=pltpu.CompilerParams(collective_id=5, has_side_effects=True, vmem_limit_bytes=60 * 1024 * 1024),
        name="block",
    )(y1, y2, c1, c2, ws, wt)


def tail_kernel(factor, xf, xs, gf, gs, chunk, xf_o, xs_o, gf_o, gs_o, space, time, rest, line):
    tm, row = lax.axis_index("tm"), lax.axis_index("row")
    for src, dst in ((xf, xf_o), (xs, xs_o), (gf, gf_o), (gs, gs_o)):
        dst[...] = src[...]
    four = chunk[4].reshape(24, 128)
    for n in range(4):
        rest[pl.ds(24 * n, 24), 0:32] = four[:, 32 * n : 32 * n + 32]
    flat = 900 * row
    start = 90 * tm % 8 + flat // 160
    main = pltpu.roll(chunk[0:4].reshape(96, 128), (96 - start) % 96, 0)
    side = pltpu.roll(rest[...], (96 - start) % 96, 0)
    for n in range(7):
        line[0:1, pl.ds(160 * n, 128)] = main[n : n + 1]
        line[0:1, pl.ds(160 * n + 128, 32)] = side[n : n + 1, 0:32]
    space[...] = pltpu.roll(line[...], (1280 - flat % 160) % 1280, 1)[0:1, 0:900] * factor
    flat = 480 * row
    start = 60 * tm % 8 + flat // 128
    main = pltpu.roll(chunk[5:8].reshape(72, 128), (72 - start) % 72, 0)
    for n in range(5):
        line[0:1, pl.ds(128 * n, 128)] = main[n : n + 1]
    time[...] = pltpu.roll(line[...], (1280 - flat % 128) % 1280, 1)[0:1, 0:480] * factor


def tail(factor, outs, chunk):
    here = pl.BlockSpec(memory_space=pltpu.VMEM)
    one = jax.ShapeDtypeStruct((2, 64, 320), BF16)
    return pl.pallas_call(
        lambda *refs: tail_kernel(factor, *refs),
        out_shape=[one] * 4 + [jax.ShapeDtypeStruct((1, 900), F32), jax.ShapeDtypeStruct((1, 480), F32)],
        in_specs=[here] * 5,
        out_specs=[here] * 6,
        scratch_shapes=[pltpu.VMEM((96, 128), F32), pltpu.VMEM((8, 1280), F32)],
        name="tail",
    )(*outs, chunk)


def per_device(output_first_half, y_second, cot_first, cot_second, weight_space, temporal_weight):
    cells_all = (
        output_first_half.shape[0]
        * output_first_half.shape[1]
        * output_first_half.shape[2]
        * lax.axis_size("tm")
        * lax.axis_size("row")
    )
    factor = 1.0 / math.sqrt(cells_all)
    flat = [v.reshape(2, 64, 320) for v in (output_first_half, y_second, cot_first, cot_second)]
    *outs, chunk = block(*flat, weight_space, temporal_weight)
    *outs, space, time = tail(factor, outs, chunk)
    return tuple(v.reshape(output_first_half.shape) for v in outs) + (space.reshape(-1), time.reshape(-1))


def solution(mesh):
    in_specs = (
        P("tm", "row", None, None),
        P("tm", "row", None, None),
        P("tm", "row", None, None),
        P("tm", "row", None, None),
        P(),
        P(),
    )
    out_specs = (
        P("tm", "row", None, None),
        P("tm", "row", None, None),
        P("tm", "row", None, None),
        P("tm", "row", None, None),
        P(("tm", "row")),
        P(("tm", "row")),
    )
    return jax.shard_map(
        per_device, mesh=mesh, in_specs=in_specs, out_specs=out_specs, check_vma=False
    )
```
